32 devices in a mesh: dp: 16 (over z, x, core), tensor: 2 (over y).
Axes of the slice: x: 2, y: 2, z: 4, core: 2. Of those that a mesh axis runs over, the one named last changes fastest.
Arguments:
- block_input: float32 [8192, 2048], P(('dp', 'tensor')), may hold values from -6 to 6
- segment_ids: int32 [16, 512], P('dp'), may hold values from 0 to 3, never falling along the last dimension, each value on 1 to 256 neighbouring positions
- cotangent: float32 [8192, 2048], P(('dp', 'tensor')), may hold values from -6 to 6
- attn_gain: float32 [2048], P('dp'), may hold values from 0.05 to 0.4
- query_weight: float32 [2048, 2048], P('dp', 'tensor'), may hold values from -0.75 to 0.75
- key_value_weight: float32 [2048, 2, 256], P('dp', None, 'tensor'), may hold values from -0.75 to 0.75
- out_weight: float32 [2048, 2048], P('dp', 'tensor'), may hold values from -0.5 to 0.5
- feed_gain: float32 [2048], P('dp'), may hold values from 0.05 to 0.4
- gate_up_weight: float32 [2048, 2, 5632], P('dp', None, 'tensor'), may hold values from -0.75 to 0.75
- down_weight: float32 [2048, 5632], P('dp', 'tensor'), may hold values from -0.078125 to 0.078125
- attn_gain_mean: float32 [2048], P('dp'), may hold values from -256 to 256
- query_weight_mean: float32 [2048, 2048], P('dp', 'tensor'), may hold values from -10 to 10
- key_value_weight_mean: float32 [2048, 2, 256], P('dp', None, 'tensor'), may hold values from -20 to 20
- out_weight_mean: float32 [2048, 2048], P('dp', 'tensor'), may hold values from -8 to 8
- feed_gain_mean: float32 [2048], P('dp'), may hold values from -112 to 112
- gate_up_weight_mean: float32 [2048, 2, 5632], P('dp', None, 'tensor'), may hold values from -1.75 to 1.75
- down_weight_mean: float32 [2048, 5632], P('dp', 'tensor'), may hold values from -16 to 16
- attn_gain_square: float32 [2048], P('dp'), may hold values from 245.76 to 1638.4
- query_weight_square: float32 [2048, 2048], P('dp', 'tensor'), may hold values from 0.393216 to 2.62144
- key_value_weight_square: float32 [2048, 2, 256], P('dp', None, 'tensor'), may hold values from 1.204224 to 8.02816
- out_weight_square: float32 [2048, 2048], P('dp', 'tensor'), may hold values from 0.221184 to 1.47456
- feed_gain_square: float32 [2048], P('dp'), may hold values from 39.3216 to 262.144
- gate_up_weight_square: float32 [2048, 2, 5632], P('dp', None, 'tensor'), may hold values from 0.00884736 to 0.0589824
- down_weight_square: float32 [2048, 5632], P('dp', 'tensor'), may hold values from 0.884736 to 5.89824
Outputs:
- block_output: float32 [8192, 2048], P(('dp', 'tensor'))
- input_grad: float32 [8192, 2048], P(('dp', 'tensor'))
- attn_gain_grad: float32 [2048], P('dp')
- query_weight_grad: float32 [2048, 2048], P('dp', 'tensor')
- key_value_weight_grad: float32 [2048, 2, 256], P('dp', None, 'tensor')
- out_weight_grad: float32 [2048, 2048], P('dp', 'tensor')
- feed_gain_grad: float32 [2048], P('dp')
- gate_up_weight_grad: float32 [2048, 2, 5632], P('dp', None, 'tensor')
- down_weight_grad: float32 [2048, 5632], P('dp', 'tensor')
- new_attn_gain: float32 [2048], P('dp')
- new_query_weight: float32 [2048, 2048], P('dp', 'tensor')
- new_key_value_weight: float32 [2048, 2, 256], P('dp', None, 'tensor')
- new_out_weight: float32 [2048, 2048], P('dp', 'tensor')
- new_feed_gain: float32 [2048], P('dp')
- new_gate_up_weight: float32 [2048, 2, 5632], P('dp', None, 'tensor')
- new_down_weight: float32 [2048, 5632], P('dp', 'tensor')
- new_attn_gain_mean: float32 [2048], P('dp')
- new_query_weight_mean: float32 [2048, 2048], P('dp', 'tensor')
- new_key_value_weight_mean: float32 [2048, 2, 256], P('dp', None, 'tensor')
- new_out_weight_mean: float32 [2048, 2048], P('dp', 'tensor')
- new_feed_gain_mean: float32 [2048], P('dp')
- new_gate_up_weight_mean: float32 [2048, 2, 5632], P('dp', None, 'tensor')
- new_down_weight_mean: float32 [2048, 5632], P('dp', 'tensor')
- new_attn_gain_square: float32 [2048], P('dp')
- new_query_weight_square: float32 [2048, 2048], P('dp', 'tensor')
- new_key_value_weight_square: float32 [2048, 2, 256], P('dp', None, 'tensor')
- new_out_weight_square: float32 [2048, 2048], P('dp', 'tensor')
- new_feed_gain_square: float32 [2048], P('dp')
- new_gate_up_weight_square: float32 [2048, 2, 5632], P('dp', None, 'tensor')
- new_down_weight_square: float32 [2048, 5632], P('dp', 'tensor')
The draws below stay inside these ranges and needn't reach their ends.
Inputs may be any that keep to these rules, and one draw needn't show every extreme that they name: In each row of segment_ids the numbers never fall and each segment holds 1 to 256 consecutive positions; some segment of every row holds exactly 256.
All inputs are finite; a program needn't handle non-finite values.
Results may differ from the reference program's by a relative error of at most 0.018.
The reference program's roundings to bfloat16 on the way count: a program that leaves them out, or rounds other values in their place, can miss the bound.
Values may be sent and summed in bfloat16 or wider, within the bound.
No kernel may reach another device: no remote copies, remote signals or barrier semaphores. Data moves between devices by JAX's collectives and lax.ppermute only.
A program may use at most 320 MiB of HBM per device.

```python
import math
import jax
import jax.numpy as jnp
import numpy as np
from jax import lax

D = 2048
HEADS = 32
KV_HEADS = 4
HEAD_DIM = 64
FF = 5632
SEQ = 512
SEQS = 16
TOKENS = 8192


def draw_query_weight(key, part):
    weight_key = jax.random.fold_in(key, 11)
    weight_scale = (D // 32) ** (-0.5)
    full_shape = (D, HEADS * HEAD_DIM)
    return jnp.clip(jax.random.normal(weight_key, full_shape, jnp.float32) * weight_scale, -6.0 * weight_scale, 6.0 * weight_scale)


def draw_key_value_weight(key, part):
    weight_key = jax.random.fold_in(key, 21)
    weight_scale = (D // 32) ** (-0.5)
    full_shape = (D, 2, KV_HEADS * HEAD_DIM)
    return jnp.clip(jax.random.normal(weight_key, full_shape, jnp.float32) * weight_scale, -6.0 * weight_scale, 6.0 * weight_scale)


def draw_block_input(key, part):
    noise_key = jax.random.fold_in(key, 31)
    return jnp.clip(jax.random.normal(noise_key, (TOKENS, D), jnp.float32), -6.0, 6.0)


def steps_of(key, dims, cuts, least, top_value):
    factor_of = 1.0
    for axis_at, blocks in cuts:
        steps = jax.random.uniform(jax.random.fold_in(jax.random.fold_in(key, 6), axis_at), (blocks,), jnp.float32, least / len(cuts), top_value / len(cuts))
        factor_of = factor_of * jnp.repeat(jnp.exp(steps), dims[axis_at] // blocks).reshape((-1,) + (1,) * (len(dims) - 1 - axis_at))
    return factor_of


def length_profile(amount, total, limit, lean):
    loads = [(1 << 20) // math.isqrt(grade ** lean) + 1 for grade in range(2, amount + 1)]
    surplus, given = total - limit - (amount - 1), [1] * (amount - 1)
    while surplus > 0:
        movable = [i for i in range(amount - 1) if given[i] < limit]
        whole, remaining = sum([loads[i] for i in movable]), surplus
        for i in movable:
            more = min(limit - given[i], max(1, remaining * loads[i] // whole), surplus)
            given[i] = given[i] + more
            surplus = surplus - more
    return np.array([limit] + given)


def ragged_sizes(key, number_of, total, limit, skew):
    if number_of == 2:
        one = jax.random.randint(key, (), max(1, total - limit), min(limit, total - 1) + 1)
        return jnp.stack([one, total - one])
    sizes = jnp.asarray(length_profile(number_of, total, limit, skew), jnp.int32)
    pairs = (number_of - 1) // 2
    donor, taker = sizes[1:1 + 2 * pairs:2], sizes[2:2 + 2 * pairs:2]
    room = jnp.minimum(donor - 1, limit - taker)
    shifted = jax.random.randint(jax.random.fold_in(key, 1), (pairs,), 0, 1 << 20) % (room + 1)
    sizes = sizes.at[1:1 + 2 * pairs:2].set(donor - shifted).at[2:2 + 2 * pairs:2].set(taker + shifted)
    return sizes[jax.random.permutation(jax.random.fold_in(key, 2), number_of)]


def noise(key, extent, deviation, most, pieces=(), held_as=jnp.bfloat16):
    array = deviation * jax.random.normal(key, extent, jnp.float32)
    if pieces:
        array = array * steps_of(key, extent, pieces, -0.22, 0.18)
    return jnp.clip(array, -most, most).astype(held_as)


def setup_inputs(seed: int = 0) -> dict:
    seeds = jax.random.split(jax.random.key(seed), 25)
    return {
        "block_input": draw_block_input(jax.random.fold_in(seeds[24], 71), 0),
        "segment_ids": jax.vmap(lambda own: jnp.searchsorted(jnp.cumsum(ragged_sizes(own, max(3, SEQ // 128), SEQ, SEQ // 2, 2)), jnp.arange(SEQ), side="right"))(jax.random.split(seeds[1], SEQS)).reshape((SEQS, SEQ)).astype(jnp.int32),
        "cotangent": noise(seeds[2], (TOKENS, D), 1.0, 6.0, ((0, 32),), jnp.float32),
        "attn_gain": jnp.clip(jnp.exp(math.log(0.4) - 2.0794415 * jax.random.uniform(seeds[3], (D,), jnp.float32) ** steps_of(seeds[3], (D,), ((0, 16),), -0.2, 0.2)), 0.05, 0.4),
        "query_weight": draw_query_weight(jax.random.fold_in(seeds[24], 71), 0),
        "key_value_weight": draw_key_value_weight(jax.random.fold_in(seeds[24], 71), 0),
        "out_weight": noise(seeds[6], (D, HEADS * HEAD_DIM), (HEADS * HEAD_DIM // 16) ** -0.5, 0.5, ((0, 16), (1, 2)), jnp.float32),
        "feed_gain": jnp.clip(jnp.exp(math.log(0.4) - 2.0794415 * jax.random.uniform(seeds[7], (D,), jnp.float32) ** steps_of(seeds[7], (D,), ((0, 16),), -0.2, 0.2)), 0.05, 0.4),
        "gate_up_weight": noise(seeds[8], (D, 2, FF), (D // 32) ** -0.5, 0.75, ((0, 16), (2, 2)), jnp.float32),
        "down_weight": noise(seeds[9], (D, FF), FF ** -0.5, 0.078125, ((0, 16), (1, 2)), jnp.float32),
        "attn_gain_mean": noise(seeds[10], (D,), (0.5 * TOKENS ** 0.5), 256.0, ((0, 16),), jnp.float32),
        "query_weight_mean": noise(seeds[11], (D, HEADS * HEAD_DIM), (0.02 * TOKENS ** 0.5), 10.0, ((0, 16), (1, 2)), jnp.float32),
        "key_value_weight_mean": noise(seeds[12], (D, 2, KV_HEADS * HEAD_DIM), (0.035 * TOKENS ** 0.5), 20.0, ((0, 16), (2, 2)), jnp.float32),
        "out_weight_mean": noise(seeds[13], (D, HEADS * HEAD_DIM), (0.015 * TOKENS ** 0.5), 8.0, ((0, 16), (1, 2)), jnp.float32),
        "feed_gain_mean": noise(seeds[14], (D,), (0.2 * TOKENS ** 0.5), 112.0, ((0, 16),), jnp.float32),
        "gate_up_weight_mean": noise(seeds[15], (D, 2, FF), (0.003 * TOKENS ** 0.5), 1.75, ((0, 16), (2, 2)), jnp.float32),
        "down_weight_mean": noise(seeds[16], (D, FF), (0.03 * TOKENS ** 0.5), 16.0, ((0, 16), (1, 2)), jnp.float32),
        "attn_gain_square": jnp.clip(jnp.exp(math.log(1638.4) - 1.89712 * jax.random.uniform(seeds[17], (D,), jnp.float32) ** steps_of(seeds[17], (D,), ((0, 16),), -0.2, 0.2)), 245.76, 1638.4),
        "query_weight_square": jnp.clip(jnp.exp(math.log(2.62144) - 1.8971199 * jax.random.uniform(seeds[18], (D, HEADS * HEAD_DIM), jnp.float32) ** steps_of(seeds[18], (D, HEADS * HEAD_DIM), ((0, 16), (1, 2)), -0.2, 0.2)), 0.393216, 2.62144),
        "key_value_weight_square": jnp.clip(jnp.exp(math.log(8.02816) - 1.89712 * jax.random.uniform(seeds[19], (D, 2, KV_HEADS * HEAD_DIM), jnp.float32) ** steps_of(seeds[19], (D, 2, KV_HEADS * HEAD_DIM), ((0, 16), (2, 2)), -0.2, 0.2)), 1.204224, 8.02816),
        "out_weight_square": jnp.clip(jnp.exp(math.log(1.47456) - 1.89712 * jax.random.uniform(seeds[20], (D, HEADS * HEAD_DIM), jnp.float32) ** steps_of(seeds[20], (D, HEADS * HEAD_DIM), ((0, 16), (1, 2)), -0.2, 0.2)), 0.221184, 1.47456),
        "feed_gain_square": jnp.clip(jnp.exp(math.log(262.144) - 1.89712 * jax.random.uniform(seeds[21], (D,), jnp.float32) ** steps_of(seeds[21], (D,), ((0, 16),), -0.2, 0.2)), 39.3216, 262.144),
        "gate_up_weight_square": jnp.clip(jnp.exp(math.log(0.0589824) - 1.89712 * jax.random.uniform(seeds[22], (D, 2, FF), jnp.float32) ** steps_of(seeds[22], (D, 2, FF), ((0, 16), (2, 2)), -0.2, 0.2)), 0.00884736, 0.0589824),
        "down_weight_square": jnp.clip(jnp.exp(math.log(5.89824) - 1.89712 * jax.random.uniform(seeds[23], (D, FF), jnp.float32) ** steps_of(seeds[23], (D, FF), ((0, 16), (1, 2)), -0.2, 0.2)), 0.884736, 5.89824),
    }


eps_norm = 1e-05
lr_rate = 0.025
beta_one = 0.9
beta_two = 0.999
adam_eps = 1e-08
decay_rate = 0.1
step_count = 2

def contract(form, left, right):
    return jnp.einsum(form, left.astype(jnp.float32), right.astype(jnp.float32), precision=lax.Precision.HIGHEST)

def norm_parts(block_rows):
    inverse = lax.rsqrt(lax.optimization_barrier(jnp.mean(block_rows * block_rows, axis=-1, keepdims=True)) + eps_norm)
    return (block_rows * inverse, inverse)

def norm_back(grad_normed, gain_value, normed, inverse):
    scaled = grad_normed * gain_value
    return inverse * (scaled - normed * lax.optimization_barrier(jnp.mean(scaled * normed, axis=-1, keepdims=True)))

def rotary_tables(segments, head_width):
    earlier = lax.optimization_barrier(jnp.sum((segments[None, :] < segments[:, None]).astype(jnp.int32), axis=1)).astype(jnp.int32)
    position = (jnp.arange(segments.shape[0], dtype=jnp.int32) - earlier).astype(jnp.float32)
    half_width = head_width // 2
    frequency = jnp.exp(jnp.arange(half_width, dtype=jnp.float32) * (-2.0 * jnp.log(10000.0) / head_width))
    angles = position[:, None] * frequency[None, :]
    angles = jnp.concatenate([angles, angles], axis=1)
    return (jnp.cos(angles), jnp.sin(angles))

def turn_half(values):
    half_width = values.shape[-1] // 2
    return jnp.concatenate([-values[..., half_width:], values[..., :half_width]], axis=-1)

def rotate(values, cosine_table, sine_table):
    return values * cosine_table + turn_half(values) * sine_table

def unrotate(values, cosine_table, sine_table):
    return values * cosine_table - turn_half(values * sine_table)

def head_forward(queries, key_rows, value_rows, allowed, score_scale):
    scores = jnp.where(allowed[None], contract('qgd,kd->gqk', queries, key_rows) * score_scale, -1e+30)
    row_max = lax.optimization_barrier(jnp.max(scores, axis=-1, keepdims=True))
    log_total = row_max + jnp.log(lax.optimization_barrier(jnp.sum(jnp.exp(scores - row_max), axis=-1, keepdims=True)))
    soft_b = jnp.where(allowed[None], jnp.exp(scores - log_total), 0.0).astype(jnp.bfloat16)
    return (contract('gqk,kd->qgd', soft_b, value_rows).astype(jnp.bfloat16), log_total[..., 0])

def head_backward(queries, key_rows, value_rows, grad_out, log_total, allowed, score_scale):
    scores = jnp.where(allowed[None], contract('qgd,kd->gqk', queries, key_rows) * score_scale, -1e+30)
    soft_weights = jnp.where(allowed[None], jnp.exp(scores - log_total[..., None]), 0.0)
    grad_soft = contract('qgd,kd->gqk', grad_out, value_rows)
    row_delta = lax.optimization_barrier(jnp.sum(soft_weights * grad_soft, axis=-1, keepdims=True))
    grad_scores = (soft_weights * (grad_soft - row_delta)).astype(jnp.bfloat16)
    grad_queries = contract('gqk,kd->qgd', grad_scores, key_rows) * score_scale
    grad_keys = contract('gqk,qgd->kd', grad_scores, queries) * score_scale
    grad_values = contract('gqk,qgd->kd', soft_weights.astype(jnp.bfloat16), grad_out)
    return (grad_queries, grad_keys, grad_values)

def attend(queries, key_rows, value_rows, allowed):
    score_scale = queries.shape[-1] ** (-0.5)

    def per_group(member):
        return head_forward(member[0], member[1], member[2], allowed, score_scale)
    outputs, log_total = lax.map(per_group, (jnp.moveaxis(queries, 1, 0), jnp.moveaxis(key_rows, 1, 0), jnp.moveaxis(value_rows, 1, 0)))
    return (jnp.moveaxis(outputs, 0, 1), log_total)

def attend_back(queries, key_rows, value_rows, grad_out, log_total, allowed):
    score_scale = queries.shape[-1] ** (-0.5)

    def per_group(member):
        return head_backward(member[0], member[1], member[2], member[3], member[4], allowed, score_scale)
    grad_queries, grad_keys, grad_values = lax.map(per_group, (jnp.moveaxis(queries, 1, 0), jnp.moveaxis(key_rows, 1, 0), jnp.moveaxis(value_rows, 1, 0), jnp.moveaxis(grad_out, 1, 0), log_total))
    return (jnp.moveaxis(grad_queries, 0, 1), jnp.moveaxis(grad_keys, 0, 1), jnp.moveaxis(grad_values, 0, 1))

def project_heads(hidden_one, query_all, key_value_all, cosine_table, sine_table, groups, group_size):
    seq_len = hidden_one.shape[0]
    queries = contract('sd,df->sf', hidden_one, query_all).reshape(seq_len, groups, group_size, HEAD_DIM)
    queries = rotate(queries, cosine_table[:, None, None, :], sine_table[:, None, None, :]).astype(jnp.bfloat16)
    key_value = contract('sd,dcf->scf', hidden_one, key_value_all)
    key_rows = rotate(key_value[:, 0].reshape(seq_len, groups, HEAD_DIM), cosine_table[:, None, :], sine_table[:, None, :]).astype(jnp.bfloat16)
    value_rows = key_value[:, 1].reshape(seq_len, groups, HEAD_DIM).astype(jnp.bfloat16)
    return (queries, key_rows, value_rows)

def adam_step(parameter, gradient, first_moment, second_moment):
    new_first = beta_one * first_moment + (1.0 - beta_one) * gradient
    new_second = beta_two * second_moment + (1.0 - beta_two) * gradient * gradient
    corrected_first = new_first / (1.0 - beta_one ** step_count)
    corrected_second = new_second / (1.0 - beta_two ** step_count)
    new_parameter = parameter - lr_rate * (corrected_first / (jnp.sqrt(corrected_second) + adam_eps) + decay_rate * parameter)
    return (new_parameter, new_first, new_second)

def sequence_pass(block_rows, segments, cot_rows, rounded):
    gain_one, query_all, key_value_all, out_all, gain_two, gate_up_all, down_all = rounded
    seq_len = block_rows.shape[0]
    groups = key_value_all.shape[2] // HEAD_DIM
    group_size = query_all.shape[1] // HEAD_DIM // groups
    index_row = jnp.arange(seq_len, dtype=jnp.int32)
    allowed = (segments[None, :] == segments[:, None]) & (index_row[None, :] <= index_row[:, None])
    cosine_table, sine_table = rotary_tables(segments, HEAD_DIM)
    normed_one, inverse_one = norm_parts(block_rows)
    hidden_one = (normed_one * gain_one.astype(jnp.float32)).astype(jnp.bfloat16)
    queries, key_rows, value_rows = project_heads(hidden_one, query_all, key_value_all, cosine_table, sine_table, groups, group_size)
    attended, log_total = attend(queries, key_rows, value_rows, allowed)
    attn_cat = attended.reshape(seq_len, -1)
    residual = block_rows + contract('sf,df->sd', attn_cat, out_all)
    normed_two, inverse_two = norm_parts(residual)
    hidden_two = (normed_two * gain_two.astype(jnp.float32)).astype(jnp.bfloat16)
    gate_up = contract('sd,dcf->scf', hidden_two, gate_up_all)
    gate_part = gate_up[:, 0]
    upward = gate_up[:, 1]
    sigmoid_gate = jax.nn.sigmoid(gate_part)
    silu_gate = gate_part * sigmoid_gate
    activated = (silu_gate * upward).astype(jnp.bfloat16)
    block_output = residual + contract('sf,df->sd', activated, down_all)
    cot_b = cot_rows.astype(jnp.bfloat16)
    down_grad = contract('sd,sf->df', cot_b, activated)
    grad_act = contract('sd,df->sf', cot_b, down_all)
    silu_slope = sigmoid_gate * (1.0 + gate_part * (1.0 - sigmoid_gate))
    grad_gate_up = jnp.stack([grad_act * upward * silu_slope, grad_act * silu_gate], axis=1).astype(jnp.bfloat16)
    gate_up_grad = contract('sd,scf->dcf', hidden_two, grad_gate_up)
    grad_hidden_two = contract('scf,dcf->sd', grad_gate_up, gate_up_all)
    grad_residual = cot_rows + norm_back(grad_hidden_two, gain_two.astype(jnp.float32), normed_two, inverse_two)
    feed_gain_grad = lax.optimization_barrier(jnp.sum(grad_hidden_two * normed_two, axis=0))
    grad_res_b = grad_residual.astype(jnp.bfloat16)
    out_grad = contract('sd,sf->df', grad_res_b, attn_cat)
    grad_cat = contract('sd,df->sf', grad_res_b, out_all).astype(jnp.bfloat16).reshape(queries.shape)
    grad_queries, grad_keys, grad_values = attend_back(queries, key_rows, value_rows, grad_cat, log_total, allowed)
    grad_query = unrotate(grad_queries, cosine_table[:, None, None, :], sine_table[:, None, None, :]).astype(jnp.bfloat16).reshape(seq_len, -1)
    grad_key_value = jnp.stack([unrotate(grad_keys, cosine_table[:, None, :], sine_table[:, None, :]).reshape(seq_len, -1), grad_values.reshape(seq_len, -1)], axis=1).astype(jnp.bfloat16)
    query_grad = contract('sd,sf->df', hidden_one, grad_query)
    key_value_grad = contract('sd,scf->dcf', hidden_one, grad_key_value)
    grad_hidden_one = contract('sf,df->sd', grad_query, query_all) + contract('scf,dcf->sd', grad_key_value, key_value_all)
    input_grad = grad_residual + norm_back(grad_hidden_one, gain_one.astype(jnp.float32), normed_one, inverse_one)
    attn_gain_grad = lax.optimization_barrier(jnp.sum(grad_hidden_one * normed_one, axis=0))
    gradients = (attn_gain_grad, query_grad, key_value_grad, out_grad, feed_gain_grad, gate_up_grad, down_grad)
    return (block_output, input_grad, gradients)

def reference(block_input, segment_ids, cotangent, attn_gain, query_weight, key_value_weight, out_weight, feed_gain, gate_up_weight, down_weight, attn_gain_mean, query_weight_mean, key_value_weight_mean, out_weight_mean, feed_gain_mean, gate_up_weight_mean, down_weight_mean, attn_gain_square, query_weight_square, key_value_weight_square, out_weight_square, feed_gain_square, gate_up_weight_square, down_weight_square):
    parameters = (attn_gain, query_weight, key_value_weight, out_weight, feed_gain, gate_up_weight, down_weight)
    firsts = (attn_gain_mean, query_weight_mean, key_value_weight_mean, out_weight_mean, feed_gain_mean, gate_up_weight_mean, down_weight_mean)
    seconds = (attn_gain_square, query_weight_square, key_value_weight_square, out_weight_square, feed_gain_square, gate_up_weight_square, down_weight_square)
    rounded = tuple((parameter.astype(jnp.bfloat16) for parameter in parameters))

    def per_sequence(running, inputs):
        block_rows, segments, cot_rows = inputs
        block_out, grad_in, gradients = sequence_pass(block_rows, segments, cot_rows, rounded)
        return (tuple((total_now + update for total_now, update in zip(running, gradients))), (block_out, grad_in))
    zeros_start = tuple((jnp.zeros(parameter.shape, jnp.float32) for parameter in parameters))
    gradients, (block_outs, grad_ins) = lax.scan(per_sequence, zeros_start, (block_input.reshape(SEQS, SEQ, D), segment_ids, cotangent.reshape(SEQS, SEQ, D)))
    updated = [adam_step(parameter, gradient, first_moment, second_moment) for parameter, gradient, first_moment, second_moment in zip(parameters, gradients, firsts, seconds)]
    new_parameters = tuple((entry[0] for entry in updated))
    new_firsts = tuple((entry[1] for entry in updated))
    new_seconds = tuple((entry[2] for entry in updated))
    return (block_outs.reshape(TOKENS, D), grad_ins.reshape(TOKENS, D)) + tuple(gradients) + new_parameters + new_firsts + new_seconds
```

```python
import jax
import jax.numpy as jnp
from jax import lax
from jax.sharding import PartitionSpec as P

HEAD_DIM = 64

eps_norm = 1e-05
lr_rate = 0.025
beta_one = 0.9
beta_two = 0.999
adam_eps = 1e-08
decay_rate = 0.1
step_count = 2


def contract(form, left, right):
    return jnp.einsum(form, left, right, preferred_element_type=jnp.float32)


def ring_order(dp_size):
    if dp_size % 2:
        return list(range(dp_size))
    chips = dp_size // 2
    width = 2 if chips <= 8 else 4
    if chips % width:
        return list(range(dp_size))
    rows = chips // width
    ring = [row * width for row in range(rows)]
    for at, row in enumerate(reversed(range(rows))):
        columns = range(1, width) if at % 2 == 0 else reversed(range(1, width))
        ring += [row * width + column for column in columns]
    return [2 * chip + core for chip in ring for core in range(2)]


def permute_blocks(values, order):
    size = values.shape[-1] // len(order)
    return jnp.concatenate([values[..., o * size : (o + 1) * size] for o in order], axis=-1)


def norm_parts(block_rows):
    inverse = lax.rsqrt(jnp.mean(block_rows * block_rows, axis=-1, keepdims=True) + eps_norm)
    return (block_rows * inverse, inverse)


def norm_back(grad_normed, gain_value, normed, inverse):
    scaled = grad_normed * gain_value
    return inverse * (scaled - normed * jnp.mean(scaled * normed, axis=-1, keepdims=True))


def rotary_tables(segments, index_row, head_width):
    earlier = jnp.sum((segments[None, :] < segments[:, None]).astype(jnp.int32), axis=1)
    position = (index_row - earlier).astype(jnp.float32)
    half_width = head_width // 2
    frequency = jnp.exp(
        jnp.arange(half_width, dtype=jnp.float32) * (-2.0 * jnp.log(10000.0) / head_width)
    )
    angles = position[:, None] * frequency[None, :]
    angles = jnp.concatenate([angles, angles], axis=1)
    return (jnp.cos(angles), jnp.sin(angles))


def turn_half(values):
    half_width = values.shape[-1] // 2
    return jnp.concatenate([-values[..., half_width:], values[..., :half_width]], axis=-1)


def rotate(values, cosine_table, sine_table):
    return values * cosine_table + turn_half(values) * sine_table


def unrotate(values, cosine_table, sine_table):
    return values * cosine_table - turn_half(values * sine_table)


def head_forward(queries, key_rows, value_rows, allowed, score_scale):
    scores = jnp.where(
        allowed[None], contract("qgd,kd->gqk", queries, key_rows) * score_scale, -1e30
    )
    row_max = jnp.max(scores, axis=-1, keepdims=True)
    log_total = row_max + jnp.log(jnp.sum(jnp.exp(scores - row_max), axis=-1, keepdims=True))
    soft_b = jnp.where(allowed[None], jnp.exp(scores - log_total), 0.0).astype(jnp.bfloat16)
    return (contract("gqk,kd->qgd", soft_b, value_rows).astype(jnp.bfloat16), log_total[..., 0])


def head_backward(queries, key_rows, value_rows, grad_out, log_total, allowed, score_scale):
    scores = jnp.where(
        allowed[None], contract("qgd,kd->gqk", queries, key_rows) * score_scale, -1e30
    )
    soft_weights = jnp.where(allowed[None], jnp.exp(scores - log_total[..., None]), 0.0)
    grad_soft = contract("qgd,kd->gqk", grad_out, value_rows)
    row_delta = jnp.sum(soft_weights * grad_soft, axis=-1, keepdims=True)
    grad_scores = (soft_weights * (grad_soft - row_delta)).astype(jnp.bfloat16)
    grad_queries = contract("gqk,kd->qgd", grad_scores, key_rows) * score_scale
    grad_keys = contract("gqk,qgd->kd", grad_scores, queries) * score_scale
    grad_values = contract("gqk,qgd->kd", soft_weights.astype(jnp.bfloat16), grad_out)
    return (grad_queries, grad_keys, grad_values)


def attend(queries, key_rows, value_rows, allowed):
    score_scale = queries.shape[-1] ** (-0.5)

    def per_group(member):
        return head_forward(member[0], member[1], member[2], allowed, score_scale)

    outputs, log_total = lax.map(
        per_group,
        (jnp.moveaxis(queries, 1, 0), jnp.moveaxis(key_rows, 1, 0), jnp.moveaxis(value_rows, 1, 0)),
    )
    return (jnp.moveaxis(outputs, 0, 1), log_total)


def attend_back(queries, key_rows, value_rows, grad_out, log_total, allowed):
    score_scale = queries.shape[-1] ** (-0.5)

    def per_group(member):
        return head_backward(
            member[0], member[1], member[2], member[3], member[4], allowed, score_scale
        )

    grad_queries, grad_keys, grad_values = lax.map(
        per_group,
        (
            jnp.moveaxis(queries, 1, 0),
            jnp.moveaxis(key_rows, 1, 0),
            jnp.moveaxis(value_rows, 1, 0),
            jnp.moveaxis(grad_out, 1, 0),
            log_total,
        ),
    )
    return (
        jnp.moveaxis(grad_queries, 0, 1),
        jnp.moveaxis(grad_keys, 0, 1),
        jnp.moveaxis(grad_values, 0, 1),
    )


def adam_step(parameter, gradient, first_moment, second_moment):
    new_first = beta_one * first_moment + (1.0 - beta_one) * gradient
    new_second = beta_two * second_moment + (1.0 - beta_two) * gradient * gradient
    corrected_first = new_first / (1.0 - beta_one**step_count)
    corrected_second = new_second / (1.0 - beta_two**step_count)
    new_parameter = parameter - lr_rate * (
        corrected_first / (jnp.sqrt(corrected_second) + adam_eps) + decay_rate * parameter
    )
    return (new_parameter, new_first, new_second)


def make_shards(dp_size, tensor_size):
    order = ring_order(dp_size)
    inverse_order = [order.index(i) for i in range(dp_size)]
    groups_of_ring = [order]

    def gather(values):
        return lax.all_gather(values, "dp", axis=0, tiled=True, axis_index_groups=groups_of_ring)

    def scatter(values):
        return lax.psum_scatter(
            values, "dp", scatter_dimension=0, tiled=True, axis_index_groups=groups_of_ring
        )

    def swap(values):
        return lax.ppermute(values, "tensor", [(0, 1), (1, 0)])

    def gather_small(values):
        at = lax.axis_index("dp")
        place = jnp.asarray(inverse_order, jnp.int32)[at]
        slots = lax.broadcasted_iota(jnp.int32, (1, dp_size, 1), 1) == place
        total = jnp.where(slots, values[:, None, :], jnp.zeros((), values.dtype))
        step = 1
        while step < dp_size:
            total = total + lax.ppermute(total, "dp", [(i, i ^ step) for i in range(dp_size)])
            step *= 2
        return total.reshape(values.shape[0], -1)

    def shards(
        block_input,
        segment_ids,
        cotangent,
        attn_gain,
        query_weight,
        key_value_weight,
        out_weight,
        feed_gain,
        gate_up_weight,
        down_weight,
        *moments,
    ):
        bf16, f32 = jnp.bfloat16, jnp.float32
        rows = attn_gain.shape[0]
        seq_len = segment_ids.shape[1]
        own = block_input.shape[0]
        heads_wide = query_weight.shape[1]
        keys_wide = key_value_weight.shape[2]
        hidden_wide = down_weight.shape[1]
        groups = keys_wide // HEAD_DIM
        group_size = heads_wide // keys_wide
        tensor_at = lax.axis_index("tensor")
        dp_at = lax.axis_index("dp")

        qkv_all = gather(
            jnp.concatenate(
                [query_weight.astype(bf16), key_value_weight.astype(bf16).reshape(rows, -1)], axis=1
            )
        )
        out_all = gather(out_weight.astype(bf16))
        gate_up_all = gather(gate_up_weight.astype(bf16).reshape(rows, -1))
        down_all = gather(down_weight.astype(bf16))
        gains = gather_small(jnp.stack([attn_gain, feed_gain]).astype(bf16)).astype(f32)
        gain_one, gain_two = gains[0:1], gains[1:2]

        block_rows = permute_blocks(block_input, order)
        cot_own = permute_blocks(cotangent, order)
        segments = jnp.roll(segment_ids[0], -tensor_at * own)
        index_row = jnp.roll(jnp.arange(seq_len, dtype=jnp.int32), -tensor_at * own)
        allowed = (segments[None, :] == segments[:, None]) & (
            index_row[None, :] <= index_row[:, None]
        )
        cosine_table, sine_table = rotary_tables(segments, index_row, HEAD_DIM)

        normed_one, inverse_one = norm_parts(block_rows)
        hidden_own = (normed_one * gain_one).astype(bf16)
        hidden_one = jnp.concatenate([hidden_own, swap(hidden_own)], axis=0)
        cot_b = cot_own.astype(bf16)
        cot_rows = jnp.concatenate([cot_b, swap(cot_b)], axis=0)

        qkv = contract("sd,df->sf", hidden_one, qkv_all)
        queries = qkv[:, :heads_wide].reshape(seq_len, groups, group_size, HEAD_DIM)
        queries = rotate(
            queries, cosine_table[:, None, None, :], sine_table[:, None, None, :]
        ).astype(bf16)
        key_rows = rotate(
            qkv[:, heads_wide : heads_wide + keys_wide].reshape(seq_len, groups, HEAD_DIM),
            cosine_table[:, None, :],
            sine_table[:, None, :],
        ).astype(bf16)
        value_rows = qkv[:, heads_wide + keys_wide :].reshape(seq_len, groups, HEAD_DIM).astype(bf16)
        attended, log_total = attend(queries, key_rows, value_rows, allowed)
        attn_cat = attended.reshape(seq_len, -1)

        def summed(form, left, right):
            theirs = swap(contract(form, left[own:], right).astype(bf16))
            return contract(form, left[:own], right) + theirs.astype(f32)

        residual = block_rows + summed("sf,df->sd", attn_cat, out_all)
        normed_two, inverse_two = norm_parts(residual)
        hidden_two_own = (normed_two * gain_two).astype(bf16)
        hidden_two = jnp.concatenate([hidden_two_own, swap(hidden_two_own)], axis=0)
        gate_up = contract("sd,df->sf", hidden_two, gate_up_all)
        gate_part = gate_up[:, :hidden_wide]
        upward = gate_up[:, hidden_wide:]
        sigmoid_gate = jax.nn.sigmoid(gate_part)
        silu_gate = gate_part * sigmoid_gate
        activated = (silu_gate * upward).astype(bf16)
        down_grad = contract("sd,sf->df", cot_rows, activated).astype(bf16)
        down_sum = scatter(down_grad)
        grad_act = contract("sd,df->sf", cot_rows, down_all)
        silu_slope = sigmoid_gate * (1.0 + gate_part * (1.0 - sigmoid_gate))
        grad_gate_up = jnp.concatenate(
            [grad_act * upward * silu_slope, grad_act * silu_gate], axis=1
        ).astype(bf16)
        gate_up_grad = contract("sd,sf->df", hidden_two, grad_gate_up).astype(bf16)
        gate_up_sum = scatter(gate_up_grad)
        block_output = residual + summed("sf,df->sd", activated, down_all)
        grad_hidden_two = summed("sf,df->sd", grad_gate_up, gate_up_all)
        grad_residual = cot_own + norm_back(grad_hidden_two, gain_two, normed_two, inverse_two)
        feed_gain_part = jnp.sum(grad_hidden_two * normed_two, axis=0)
        grad_rows_own = grad_residual.astype(bf16)
        grad_rows = jnp.concatenate([grad_rows_own, swap(grad_rows_own)], axis=0)
        out_grad = contract("sd,sf->df", grad_rows, attn_cat).astype(bf16)
        out_sum = scatter(out_grad)
        grad_cat = contract("sd,df->sf", grad_rows, out_all).astype(bf16).reshape(queries.shape)
        grad_queries, grad_keys, grad_values = attend_back(
            queries, key_rows, value_rows, grad_cat, log_total, allowed
        )
        grad_query = (
            unrotate(grad_queries, cosine_table[:, None, None, :], sine_table[:, None, None, :])
            .astype(bf16)
            .reshape(seq_len, -1)
        )
        grad_keys = unrotate(grad_keys, cosine_table[:, None, :], sine_table[:, None, :])
        grad_qkv = jnp.concatenate(
            [
                grad_query,
                grad_keys.reshape(seq_len, -1).astype(bf16),
                grad_values.reshape(seq_len, -1).astype(bf16),
            ],
            axis=1,
        )
        qkv_grad = contract("sd,sf->df", hidden_one, grad_qkv).astype(bf16)
        grad_hidden_one = summed("sf,df->sd", grad_qkv, qkv_all)
        input_grad = grad_residual + norm_back(grad_hidden_one, gain_one, normed_one, inverse_one)
        attn_gain_part = jnp.sum(grad_hidden_one * normed_one, axis=0)

        gain_parts = jnp.stack([attn_gain_part, feed_gain_part])
        gain_parts = gain_parts + swap(gain_parts)
        high = gain_parts.astype(bf16)
        low = (gain_parts - high.astype(f32)).astype(bf16)
        terms = [high[0], low[0], high[1], low[1]]
        wide = -(-len(terms) * dp_size // 128) * 128
        lane = lax.broadcasted_iota(jnp.int32, (1, wide), 1)
        gain_columns = jnp.zeros((terms[0].shape[0], wide), bf16)
        for at, term in enumerate(terms):
            gain_columns = jnp.where(lane == at * dp_size + dp_at, term[:, None], gain_columns)
        last_sum = scatter(jnp.concatenate([qkv_grad, gain_columns], axis=1))

        query_sum = last_sum[:, :heads_wide].astype(f32)
        key_value_sum = (
            last_sum[:, heads_wide : heads_wide + 2 * keys_wide]
            .astype(f32)
            .reshape(key_value_weight.shape)
        )
        gain_sums = last_sum[:, heads_wide + 2 * keys_wide :].astype(f32)
        attn_gain_sum = jnp.sum(gain_sums[:, : 2 * dp_size], axis=1)
        feed_gain_sum = jnp.sum(gain_sums[:, 2 * dp_size : 4 * dp_size], axis=1)

        parameters = (
            attn_gain,
            query_weight,
            key_value_weight,
            out_weight,
            feed_gain,
            gate_up_weight,
            down_weight,
        )
        gradients = (
            attn_gain_sum,
            query_sum,
            key_value_sum,
            out_sum.astype(f32),
            feed_gain_sum,
            gate_up_sum.astype(f32).reshape(gate_up_weight.shape),
            down_sum.astype(f32),
        )
        count = len(parameters)
        updated = [
            adam_step(parameter, gradient, first_moment, second_moment)
            for parameter, gradient, first_moment, second_moment in zip(
                parameters, gradients, moments[:count], moments[count:]
            )
        ]
        return (
            (
                permute_blocks(block_output, inverse_order),
                permute_blocks(input_grad, inverse_order),
            )
            + gradients
            + tuple(entry[0] for entry in updated)
            + tuple(entry[1] for entry in updated)
            + tuple(entry[2] for entry in updated)
        )

    return shards


def solution(mesh):
    tokens = P(("dp", "tensor"), None)
    gain = P("dp")
    flat = P("dp", "tensor")
    paired = P("dp", None, "tensor")
    weights = (gain, flat, paired, flat, gain, paired, flat)
    return jax.shard_map(
        make_shards(mesh.shape["dp"], mesh.shape["tensor"]),
        mesh=mesh,
        in_specs=(tokens, P("dp", None), tokens) + weights * 3,
        out_specs=(tokens, tokens) + weights * 4,
        check_vma=False,
    )
```

```python
import jax
import jax.numpy as jnp
from jax import lax
from jax.experimental import pallas as pl
from jax.experimental.pallas import tpu as pltpu
from jax.experimental.layout import Layout, with_layout_constraint
from jax.sharding import PartitionSpec as P


HEAD_DIM = 64

eps_norm = 1e-05
lr_rate = 0.025
beta_one = 0.9
beta_two = 0.999
adam_eps = 1e-08
decay_rate = 0.1
step_count = 2


def rows_major(values):
    return with_layout_constraint(values, Layout(major_to_minor=(0, 1)))


def ring_order(dp_size):
    if dp_size % 2:
        return list(range(dp_size))
    chips = dp_size // 2
    width = 2 if chips <= 8 else 4
    if chips % width:
        return list(range(dp_size))
    rows = chips // width
    ring = [row * width for row in range(rows)]
    for at, row in enumerate(reversed(range(rows))):
        columns = range(1, width) if at % 2 == 0 else reversed(range(1, width))
        ring += [row * width + column for column in columns]
    return [2 * chip + core for core in range(2) for chip in ring]


def permute_blocks(values, order):
    size = values.shape[-1] // len(order)
    if size % 128:
        parts = [values[..., o * size : (o + 1) * size] for o in order]
        return jnp.concatenate(parts, axis=-1)

    def body(values_ref, out_ref):
        for at, o in enumerate(order):
            out_ref[:, at * size : (at + 1) * size] = values_ref[:, o * size : (o + 1) * size]

    rows = values.shape[0] // 4
    spec = pl.BlockSpec((rows, values.shape[1]), lambda i: (i, 0))
    return pl.pallas_call(
        body,
        grid=(4,),
        in_specs=[spec],
        out_specs=spec,
        out_shape=jax.ShapeDtypeStruct(values.shape, values.dtype),
        cost_estimate=pl.CostEstimate(
            flops=0, transcendentals=0, bytes_accessed=2 * values.size * values.dtype.itemsize
        ),
    )(values)


def norm_parts(block_rows):
    inverse = lax.rsqrt(jnp.mean(block_rows * block_rows, axis=-1, keepdims=True) + eps_norm)
    return (block_rows * inverse, inverse)


def norm_back(grad_normed, gain_value, normed, inverse):
    scaled = grad_normed * gain_value
    return inverse * (scaled - normed * jnp.mean(scaled * normed, axis=-1, keepdims=True))


def rotary_tables(segments, head_width, first):
    earlier = jnp.sum((segments[None, :] < segments[:, None]).astype(jnp.int32), axis=1)
    position = jnp.arange(segments.shape[0], dtype=jnp.int32) - earlier
    half = segments.shape[0] // 2
    position = jnp.where(first == 0, position, jnp.concatenate([position[half:], position[:half]]))
    half_width = head_width // 2
    frequency = jnp.exp(
        jnp.arange(half_width, dtype=jnp.float32) * (-2.0 * jnp.log(10000.0) / head_width)
    )
    angles = position.astype(jnp.float32)[:, None] * frequency[None, :]
    angles = jnp.concatenate([angles] * 4, axis=1)
    return (jnp.cos(angles), jnp.sin(angles))


def nt_dot(left, right):
    return lax.dot_general(
        left, right, (((1,), (1,)), ((), ())), preferred_element_type=jnp.float32
    )


def plain_dot(left, right):
    return jnp.dot(left, right, preferred_element_type=jnp.float32)


def key_span(block):
    return max(0, block - 2), block + 1


def pair_mask(seg_column, seg_row, first, last, block, size):
    shape = ((last - first) * size, size)
    keys = lax.broadcasted_iota(jnp.int32, shape, 0) + first * size
    rows = lax.broadcasted_iota(jnp.int32, shape, 1) + block * size
    same = seg_column[first * size : last * size, :] == seg_row[:, block * size : (block + 1) * size]
    return same & (keys <= rows)


def both_sides(values, low):
    zero = jnp.zeros_like(values)
    left_first, right_second = jnp.where(low, values, zero), jnp.where(low, zero, values)
    return (
        (left_first, pltpu.roll(left_first, HEAD_DIM, 1)),
        (pltpu.roll(right_second, HEAD_DIM, 1), right_second),
    )


def attend_body(
    at_ref,
    qkv_ref,
    cos_ref,
    sin_ref,
    seg_column_ref,
    seg_row_ref,
    out_ref,
    query_ref,
    side_ref,
    key_ref,
    value_ref,
    log_ref,
    value_turned,
):
    bf16, f32 = jnp.bfloat16, jnp.float32
    seq_len, wide = out_ref.shape
    size, twice = seq_len // 4, 2 * HEAD_DIM
    half = HEAD_DIM // 2
    pairs = wide // twice
    scale = HEAD_DIM ** (-0.5)
    at = at_ref[0]
    lane = lax.broadcasted_iota(jnp.int32, (1, twice), 1)
    low, front = lane < HEAD_DIM, lane % HEAD_DIM < half

    def place(block):
        return pl.ds(pl.multiple_of((block + 2 * at) % 4 * size, size), size)

    def turned(values, rows):
        back = pltpu.roll(values, twice - half, 1)
        ahead = pltpu.roll(values, half, 1)
        return values * cos_ref[rows, :] + jnp.where(front, -back, ahead) * sin_ref[rows, :]

    for block in range(4):
        rows, natural = place(block), slice(block * size, (block + 1) * size)
        keys = turned(qkv_ref[rows, wide : wide + twice], rows).astype(bf16)
        values = qkv_ref[rows, wide + twice : wide + 2 * twice].astype(bf16)
        key_ref[natural, :] = keys
        value_ref[natural, :] = values
        for group, sides in enumerate(both_sides(keys.astype(f32), low)):
            for side in range(2):
                side_ref[group, side, natural, :] = sides[side].astype(bf16)
        value_turned[:, natural] = values.astype(f32).T.astype(bf16)

    def pair_step(pair, carry):
        lanes = pl.ds(pl.multiple_of(pair * twice, twice), twice)
        group = pair // (pairs // 2)
        for block in range(4):
            first, last = key_span(block)
            span = slice(first * size, last * size)
            rows = place(block)
            queries = turned(qkv_ref[rows, lanes], rows).astype(bf16)
            query_ref[rows, lanes] = queries
            mask = pair_mask(seg_column_ref, seg_row_ref, first, last, block, size)
            soft = []
            for side in range(2):
                scores = nt_dot(side_ref[group, side, span, :], queries) * scale
                scores = jnp.where(mask, scores, -1e30)
                top = jnp.max(scores, axis=0, keepdims=True)
                powers = jnp.exp(scores - top)
                total = jnp.sum(powers, axis=0, keepdims=True)
                log_ref[pair, side : side + 1, block * size : (block + 1) * size] = top + jnp.log(total)
                soft.append((powers * (1.0 / total)).astype(bf16))
            weights = value_turned[pl.ds(pl.multiple_of(group * HEAD_DIM, HEAD_DIM), HEAD_DIM), span]
            result = plain_dot(weights, jnp.concatenate(soft, axis=1))
            result = jnp.concatenate([result[:, :size], result[:, size:]], axis=0)
            out_ref[rows, lanes] = result.T.astype(bf16)
        return carry

    lax.fori_loop(0, pairs, pair_step, 0)


def attend_back_body(
    at_ref,
    grad_ref,
    query_ref,
    side_ref,
    key_ref,
    value_ref,
    log_ref,
    cos_ref,
    sin_ref,
    cos_turned_ref,
    sin_turned_ref,
    seg_column_ref,
    seg_row_ref,
    out_ref,
    value_side,
    key_turned,
    key_total,
    value_total,
):
    bf16, f32 = jnp.bfloat16, jnp.float32
    seq_len, wide = query_ref.shape
    size, twice = seq_len // 4, 2 * HEAD_DIM
    half = HEAD_DIM // 2
    pairs = wide // twice
    scale = HEAD_DIM ** (-0.5)
    at = at_ref[0]
    lane = lax.broadcasted_iota(jnp.int32, (1, twice), 1)
    low, front = lane < HEAD_DIM, lane % HEAD_DIM < half

    def place(block):
        return pl.ds(pl.multiple_of((block + 2 * at) % 4 * size, size), size)

    for block in range(4):
        natural = slice(block * size, (block + 1) * size)
        for group, sides in enumerate(both_sides(value_ref[natural, :].astype(f32), low)):
            for side in range(2):
                value_side[group, side, natural, :] = sides[side].astype(bf16)
        key_turned[:, natural] = key_ref[natural, :].astype(f32).T.astype(bf16)
    key_total[...] = jnp.zeros_like(key_total)
    value_total[...] = jnp.zeros_like(value_total)

    def split(values):
        zero = jnp.zeros_like(values)
        return jnp.concatenate([jnp.where(low, values, zero), jnp.where(low, zero, values)], axis=0)

    def pair_step(pair, carry):
        lanes = pl.ds(pl.multiple_of(pair * twice, twice), twice)
        group = pair // (pairs // 2)
        for block in range(4):
            first, last = key_span(block)
            span = slice(first * size, last * size)
            rows = place(block)
            queries, grads = query_ref[rows, lanes], grad_ref[rows, lanes]
            mask = pair_mask(seg_column_ref, seg_row_ref, first, last, block, size)
            soft, slopes = [], []
            for side in range(2):
                scores = nt_dot(side_ref[group, side, span, :], queries) * scale
                logs = log_ref[pair, side : side + 1, block * size : (block + 1) * size]
                weights = jnp.exp(jnp.where(mask, scores, -1e30) - logs)
                grad_soft = nt_dot(value_side[group, side, span, :], grads)
                delta = jnp.sum(weights * grad_soft, axis=0, keepdims=True)
                slopes.append((weights * (grad_soft - delta)).astype(bf16))
                soft.append(weights.astype(bf16))
            slopes, soft = jnp.concatenate(slopes, axis=1), jnp.concatenate(soft, axis=1)
            key_total[group, span, :] += plain_dot(slopes, split(queries))
            value_total[group, span, :] += plain_dot(soft, split(grads))
            keys = key_turned[pl.ds(pl.multiple_of(group * HEAD_DIM, HEAD_DIM), HEAD_DIM), span]
            result = plain_dot(keys, slopes) * scale
            cosine, sine = cos_turned_ref[:, rows], sin_turned_ref[:, rows]
            parts = []
            for side in range(2):
                own = result[:, side * size : (side + 1) * size]
                turn = own * sine
                own = own * cosine
                parts += [own[:half] + turn[half:], own[half:] - turn[:half]]
            out_ref[rows, lanes] = jnp.concatenate(parts, axis=0).T.astype(bf16)
        return carry

    lax.fori_loop(0, pairs, pair_step, 0)

    for block in range(4):
        rows, natural = place(block), slice(block * size, (block + 1) * size)
        folded = []
        for total in (key_total, value_total):
            groups = [total[group, natural, :] for group in range(2)]
            groups = [part + pltpu.roll(part, HEAD_DIM, 1) for part in groups]
            folded.append(jnp.where(low, groups[0], groups[1]))
        keys = folded[0] * scale
        turn = keys * sin_ref[rows, :]
        back, ahead = pltpu.roll(turn, twice - half, 1), pltpu.roll(turn, half, 1)
        keys = keys * cos_ref[rows, :] + jnp.where(front, back, -ahead)
        out_ref[rows, wide : wide + twice] = keys.astype(bf16)
        out_ref[rows, wide + twice : wide + 2 * twice] = folded[1].astype(bf16)


def whole_specs(count):
    return [pl.BlockSpec(memory_space=pltpu.SMEM)] + [pl.BlockSpec(memory_space=pltpu.VMEM)] * count


def attend(tensor_at, qkv, cosine, sine, segments, heads_wide):
    seq_len, bf16, f32 = qkv.shape[0], jnp.bfloat16, jnp.float32
    twice = 2 * HEAD_DIM
    shapes = (
        ((seq_len, heads_wide), bf16),
        ((seq_len, heads_wide), bf16),
        ((2, 2, seq_len, twice), bf16),
        ((seq_len, twice), bf16),
        ((seq_len, twice), bf16),
        ((heads_wide // twice, 2, seq_len), f32),
    )
    work = heads_wide * seq_len * seq_len
    return pl.pallas_call(
        attend_body,
        in_specs=whole_specs(5),
        out_specs=[pl.BlockSpec(memory_space=pltpu.VMEM)] * len(shapes),
        out_shape=[jax.ShapeDtypeStruct(shape, kind) for shape, kind in shapes],
        scratch_shapes=[pltpu.VMEM((twice, seq_len), bf16)],
        cost_estimate=pl.CostEstimate(
            flops=4 * work, transcendentals=work // HEAD_DIM, bytes_accessed=8 * qkv.size
        ),
    )(tensor_at[None], qkv, cosine, sine, segments[:, None], segments[None, :])


def attend_back(tensor_at, grad_cat, saved, cosine, sine, segments):
    queries, sides, keys, values, logs = saved
    (seq_len, heads_wide), bf16, f32 = queries.shape, jnp.bfloat16, jnp.float32
    twice = 2 * HEAD_DIM
    work = heads_wide * seq_len * seq_len
    return pl.pallas_call(
        attend_back_body,
        in_specs=whole_specs(12),
        out_specs=pl.BlockSpec(memory_space=pltpu.VMEM),
        out_shape=jax.ShapeDtypeStruct((seq_len, heads_wide + 2 * twice), bf16),
        scratch_shapes=[
            pltpu.VMEM((2, 2, seq_len, twice), bf16),
            pltpu.VMEM((twice, seq_len), bf16),
            pltpu.VMEM((2, seq_len, twice), f32),
            pltpu.VMEM((2, seq_len, twice), f32),
        ],
        cost_estimate=pl.CostEstimate(
            flops=10 * work, transcendentals=work // HEAD_DIM, bytes_accessed=8 * queries.size
        ),
    )(
        tensor_at[None],
        grad_cat,
        queries,
        sides,
        keys,
        values,
        logs,
        cosine,
        sine,
        cosine[:, :HEAD_DIM].T,
        sine[:, :HEAD_DIM].T,
        segments[:, None],
        segments[None, :],
    )


def cost_of(flops, *arrays):
    moved = sum(array.size * jnp.dtype(array.dtype).itemsize for array in arrays)
    return pl.CostEstimate(flops=flops, transcendentals=0, bytes_accessed=moved)


def tile_of(columns, most=256):
    return next(size for size in range(most, 0, -128) if columns % size == 0)


def by_rows(rows, step, chunk=256):
    chunk = min(chunk, rows)

    def one(at, carry):
        step(pl.ds(pl.multiple_of(at * chunk, chunk), chunk))
        return carry

    lax.fori_loop(0, rows // chunk, one, 0)


def times(left, right, first, columns, kind):
    rows, depth = left.shape
    tile = tile_of(columns)
    shape = jax.ShapeDtypeStruct((rows, columns), kind)

    def body(left_ref, right_ref, out_ref):
        def step(at):
            out_ref[at, :] = plain_dot(left_ref[at, :], right_ref[...]).astype(out_ref.dtype)

        by_rows(rows, step)

    return pl.pallas_call(
        body,
        grid=(columns // tile,),
        in_specs=[
            pl.BlockSpec((rows, depth), lambda j: (0, 0)),
            pl.BlockSpec((depth, tile), lambda j: (0, j + first // tile)),
        ],
        out_specs=pl.BlockSpec((rows, tile), lambda j: (0, j)),
        out_shape=shape,
        cost_estimate=cost_of(2 * rows * depth * columns, left, shape),
    )(left, right)


def times_turned(left, at, right, first, kind):
    stack = left if left.ndim == 3 else left[None]
    parts, rows, depth = stack.shape
    rows //= 2
    count, wide = right.shape
    tile = tile_of(count, 512)

    def body(left_ref, right_ref, out_ref):
        def step(rows_at):
            total = 0.0
            for part in range(parts):
                begin = first + part * depth
                total += nt_dot(left_ref[part, rows_at, :], right_ref[:, begin : begin + depth])
            out_ref[rows_at, :] = total.astype(out_ref.dtype)

        by_rows(rows, step)

    shape = jax.ShapeDtypeStruct((rows, count), kind)
    return pl.pallas_call(
        body,
        grid=(count // tile,),
        in_specs=[
            pl.BlockSpec((parts, rows, depth), lambda j: (0, at, 0)),
            pl.BlockSpec((tile, wide), lambda j: (j, 0)),
        ],
        out_specs=pl.BlockSpec((rows, tile), lambda j: (0, j)),
        out_shape=shape,
        cost_estimate=cost_of(2 * rows * depth * parts * count, right, shape),
    )(stack, right)


def turned_times(left, half, right, received=None):
    stack = right if right.ndim == 3 else right[None]
    parts, tokens, columns = stack.shape
    count = left.shape[1] // 2
    tile = tile_of(columns, max(512, columns // 2))
    tiles = columns // tile

    def body(half_ref, left_ref, right_ref, *rest):
        *received_ref, out_ref, turned = rest

        @pl.when(pl.program_id(0) == 0)
        def _():
            def turn(at, carry):
                columns_at = pl.ds(pl.multiple_of(at * 128, 128), 128)
                turned[columns_at, :] = left_ref[:, columns_at].astype(jnp.float32).T.astype(jnp.bfloat16)
                return carry

            lax.fori_loop(0, count // 128, turn, 0)

        def step(at):
            total = plain_dot(turned[at, :], right_ref[0])
            if received_ref:
                total += received_ref[0][at, :].astype(jnp.float32)
            out_ref[at, :] = total.astype(jnp.bfloat16)

        by_rows(count, step)

    block = pl.BlockSpec((count, tile), lambda j, half_ref: (0, j))
    shape = jax.ShapeDtypeStruct((count, parts * columns), jnp.bfloat16)
    more = [] if received is None else [received]
    return pl.pallas_call(
        body,
        grid_spec=pltpu.PrefetchScalarGridSpec(
            num_scalar_prefetch=1,
            grid=(parts * tiles,),
            in_specs=[
                pl.BlockSpec((tokens, count), lambda j, half_ref: (0, half_ref[0])),
                pl.BlockSpec((1, tokens, tile), lambda j, half_ref: (j // tiles, 0, j % tiles)),
            ]
            + [block] * len(more),
            out_specs=block,
            scratch_shapes=[pltpu.VMEM((count, tokens), jnp.bfloat16)],
        ),
        out_shape=shape,
        cost_estimate=cost_of(2 * tokens * count * parts * columns, stack, shape, *more),
    )(half[None], left, stack, *more)


def feed_forward(hidden, gate_up_all):
    rows, depth = hidden.shape
    wide = gate_up_all.shape[1] // 2
    tile = tile_of(wide)

    def body(hidden_ref, gate_ref, up_ref, gate_out, up_out, active_out):
        def step(at):
            gate_part = plain_dot(hidden_ref[at, :], gate_ref[...])
            upward = plain_dot(hidden_ref[at, :], up_ref[...])
            gate_out[at, :] = gate_part
            up_out[at, :] = upward
            active_out[at, :] = (gate_part * jax.nn.sigmoid(gate_part) * upward).astype(jnp.bfloat16)

        by_rows(rows, step)

    block = pl.BlockSpec((rows, tile), lambda j: (0, j))
    kinds = (jnp.float32, jnp.float32, jnp.bfloat16)
    shapes = [jax.ShapeDtypeStruct((rows, wide), kind) for kind in kinds]
    return pl.pallas_call(
        body,
        grid=(wide // tile,),
        in_specs=[
            pl.BlockSpec((rows, depth), lambda j: (0, 0)),
            pl.BlockSpec((depth, tile), lambda j: (0, j)),
            pl.BlockSpec((depth, tile), lambda j: (0, j + wide // tile)),
        ],
        out_specs=[block] * 3,
        out_shape=shapes,
        cost_estimate=cost_of(4 * rows * depth * wide, gate_up_all, *shapes),
    )(hidden, gate_up_all, gate_up_all)


def feed_forward_back(cot, down_all, gate_part, upward):
    rows, depth = cot.shape
    wide = down_all.shape[1]
    tile = tile_of(wide, wide // 2)

    def body(cot_ref, down_ref, gate_ref, up_ref, out_ref):
        def step(at):
            grad_act = plain_dot(cot_ref[at, :], down_ref[...])
            gate = gate_ref[at, :]
            sigmoid_gate = jax.nn.sigmoid(gate)
            slope = sigmoid_gate * (1.0 + gate * (1.0 - sigmoid_gate))
            out_ref[0, at, :] = (grad_act * up_ref[at, :] * slope).astype(jnp.bfloat16)
            out_ref[1, at, :] = (grad_act * (gate * sigmoid_gate)).astype(jnp.bfloat16)

        by_rows(rows, step)

    block = pl.BlockSpec((rows, tile), lambda j: (0, j))
    shape = jax.ShapeDtypeStruct((2, rows, wide), jnp.bfloat16)
    return pl.pallas_call(
        body,
        grid=(wide // tile,),
        in_specs=[
            pl.BlockSpec((rows, depth), lambda j: (0, 0)),
            pl.BlockSpec((depth, tile), lambda j: (0, j)),
            block,
            block,
        ],
        out_specs=pl.BlockSpec((2, rows, tile), lambda j: (0, 0, j)),
        out_shape=shape,
        cost_estimate=cost_of(2 * rows * depth * wide, down_all, gate_part, upward, shape),
    )(cot, down_all, gate_part, upward)


def adam_step(parameter, gradient, first_moment, second_moment):
    new_first = beta_one * first_moment + (1.0 - beta_one) * gradient
    new_second = beta_two * second_moment + (1.0 - beta_two) * gradient * gradient
    corrected_first = new_first / (1.0 - beta_one**step_count)
    corrected_second = new_second / (1.0 - beta_two**step_count)
    new_parameter = parameter - lr_rate * (
        corrected_first / (jnp.sqrt(corrected_second) + adam_eps) + decay_rate * parameter
    )
    return (new_parameter, new_first, new_second)


def adam_update(gradient, parameters, firsts, seconds):
    rows = gradient.shape[0]
    chunk = min(rows, 16)
    count = len(parameters)

    def body(gradient_ref, *refs):
        old, new = refs[: 3 * count], refs[3 * count :]
        begin = 0
        for at in range(count):
            shape = old[3 * at].shape
            middle = range(shape[1]) if len(shape) == 3 else (None,)
            for part in middle:
                wide = shape[-1]
                where = (slice(None), slice(None)) if part is None else (slice(None), part, slice(None))
                grads = gradient_ref[:, begin : begin + wide].astype(jnp.float32)
                begin += wide
                results = adam_step(
                    old[3 * at][where], grads, old[3 * at + 1][where], old[3 * at + 2][where]
                )
                new[4 * at][where] = grads
                for index, result in enumerate(results):
                    new[4 * at + 1 + index][where] = result

    def spec(array):
        return pl.BlockSpec(
            (chunk,) + array.shape[1:], lambda i, zeros=(0,) * (array.ndim - 1): (i,) + zeros
        )

    inputs = [array for group in zip(parameters, firsts, seconds) for array in group]
    outputs = [array for array in parameters for _ in range(4)]
    results = pl.pallas_call(
        body,
        grid=(rows // chunk,),
        in_specs=[spec(gradient)] + [spec(array) for array in inputs],
        out_specs=[spec(array) for array in outputs],
        out_shape=[jax.ShapeDtypeStruct(array.shape, jnp.float32) for array in outputs],
        cost_estimate=cost_of(20 * gradient.size, *inputs, *outputs),
    )(gradient, *inputs)
    return [results[4 * at : 4 * at + 4] for at in range(count)]


def make_shards(dp_size):
    order = ring_order(dp_size)
    inverse_order = [order.index(i) for i in range(dp_size)]
    chips = dp_size // 2
    rings = [order[:chips], order[chips:]]

    def gather(values):
        return lax.all_gather(values, "dp", axis=0, tiled=True, axis_index_groups=[order])

    def scatter(values):
        return lax.psum_scatter(
            values, "dp", scatter_dimension=0, tiled=True, axis_index_groups=rings
        )

    def swap_core(values):
        return lax.ppermute(values, "dp", [(i, i ^ 1) for i in range(dp_size)])

    def pair_grad(left, right):
        core = lax.axis_index("dp") % 2
        other = turned_times(left, 1 - core, right)
        received = swap_core(other)
        return turned_times(left, core, right, received)

    def swap(values):
        return lax.ppermute(values, "tensor", [(0, 1), (1, 0)])

    def gather_small(values):
        at = lax.axis_index("dp")
        place = jnp.asarray(inverse_order, jnp.int32)[at]
        slots = lax.broadcasted_iota(jnp.int32, (1, dp_size, 1), 1) == place
        total = jnp.where(slots, values[:, None, :], jnp.zeros((), values.dtype))
        step = 1
        while step < dp_size:
            total = total + lax.ppermute(total, "dp", [(i, i ^ step) for i in range(dp_size)])
            step *= 2
        return total.reshape(values.shape[0], -1)

    def shards(
        block_input,
        segment_ids,
        cotangent,
        attn_gain,
        query_weight,
        key_value_weight,
        out_weight,
        feed_gain,
        gate_up_weight,
        down_weight,
        *moments,
    ):
        bf16, f32 = jnp.bfloat16, jnp.float32
        rows = attn_gain.shape[0]
        own = block_input.shape[0]
        heads_wide = query_weight.shape[1]
        keys_wide = key_value_weight.shape[2]
        tensor_at = lax.axis_index("tensor")

        qkv_wide = heads_wide + 2 * keys_wide
        gains = gather_small(jnp.stack([attn_gain, feed_gain]).astype(bf16)).astype(f32)
        attn_all = gather(
            jnp.concatenate(
                [query_weight.astype(bf16), key_value_weight.astype(bf16).reshape(rows, -1), out_weight.astype(bf16)],
                axis=1,
            )
        )
        gate_up_all = gather(gate_up_weight.astype(bf16).reshape(rows, -1))
        down_all = gather(down_weight.astype(bf16))
        gain_one, gain_two = gains[0:1], gains[1:2]

        block_rows = permute_blocks(block_input, order)
        cot_own = permute_blocks(cotangent, order)
        segments = segment_ids[0]
        cosine_table, sine_table = rotary_tables(segments, HEAD_DIM, tensor_at * own)

        def both(values):
            return jnp.concatenate([values, swap(values)], axis=0)

        def summed(left, right, first):
            partial = times_turned(left, 1, right, first, bf16)
            theirs = swap(partial)
            mine = times_turned(left, 0, right, first, f32)
            return mine + theirs.astype(f32)

        normed_one, inverse_one = norm_parts(block_rows)
        hidden_one = both((normed_one * gain_one).astype(bf16))
        cot_rows = both(cot_own.astype(bf16))

        qkv = times(hidden_one, attn_all, 0, qkv_wide, f32)
        attn_cat, *saved = attend(
            tensor_at, qkv, cosine_table, sine_table, segments, heads_wide
        )

        residual = block_rows + summed(attn_cat, attn_all, qkv_wide)
        normed_two, inverse_two = norm_parts(residual)
        hidden_two = both((normed_two * gain_two).astype(bf16))
        gate_part, upward, activated = feed_forward(hidden_two, gate_up_all)
        down_grad = pair_grad(cot_rows, activated)
        down_grad, down_all = lax.optimization_barrier((down_grad, down_all))
        down_sum = scatter(down_grad)
        grad_gate_up = feed_forward_back(cot_rows, down_all, gate_part, upward)
        grad_hidden_two = summed(grad_gate_up, gate_up_all, 0)
        gate_up_grad = pair_grad(hidden_two, grad_gate_up)
        gate_up_sum = scatter(gate_up_grad)
        feed_sum = summed(activated, down_all, 0)
        block_output = lax.optimization_barrier(residual) + feed_sum
        grad_residual = cot_own + norm_back(grad_hidden_two, gain_two, normed_two, inverse_two)
        feed_gain_part = jnp.sum(grad_hidden_two * normed_two, axis=0)
        grad_rows = both(grad_residual.astype(bf16))
        out_grad = pair_grad(grad_rows, attn_cat)
        grad_cat = times(grad_rows, attn_all, qkv_wide, heads_wide, bf16)
        grad_qkv = attend_back(
            tensor_at, grad_cat, saved, cosine_table, sine_table, segments
        )
        grad_hidden_one = summed(grad_qkv, attn_all, 0)
        qkv_grad = pair_grad(hidden_one, grad_qkv)
        input_grad = grad_residual + norm_back(grad_hidden_one, gain_one, normed_one, inverse_one)
        attn_gain_part = jnp.sum(grad_hidden_one * normed_one, axis=0)

        parts = [rows_major(qkv_grad), rows_major(out_grad)]
        attn_sum = rows_major(scatter(jnp.concatenate(parts, axis=1)))
        gain_parts = jnp.stack([attn_gain_part, feed_gain_part])
        gain_parts = gain_parts + swap(gain_parts)
        step = 1
        while step < dp_size:
            pairs = [(i, i ^ step) for i in range(dp_size)]
            gain_parts = gain_parts + lax.ppermute(gain_parts, "dp", pairs)
            step *= 2
        place = jnp.asarray(inverse_order, jnp.int32)[lax.axis_index("dp")]
        gain_sums = lax.dynamic_slice(gain_parts, (0, place * rows), (2, rows))
        attn_gain_sum, feed_gain_sum = gain_sums[0], gain_sums[1]

        count = len(moments) // 2
        firsts, seconds = moments[:count], moments[count:]

        def update(gradient, parameters, places):
            results = adam_update(gradient, parameters, [firsts[at] for at in places], [seconds[at] for at in places])
            return dict(zip(places, results))

        attn_parameters = (query_weight, key_value_weight, out_weight)
        results = update(down_sum, (down_weight,), (6,))
        results |= update(gate_up_sum, (gate_up_weight,), (5,))
        results |= update(attn_sum, attn_parameters, (1, 2, 3))
        for at, parameter, gradient in (
            (0, attn_gain, attn_gain_sum),
            (4, feed_gain, feed_gain_sum),
        ):
            results[at] = (gradient, *adam_step(parameter, gradient, firsts[at], seconds[at]))
        return (
            permute_blocks(block_output, inverse_order),
            permute_blocks(input_grad, inverse_order),
        ) + tuple(results[at][kind] for kind in range(4) for at in range(count))

    return shards


def solution(mesh):
    tokens = P(("dp", "tensor"), None)
    gain = P("dp")
    flat = P("dp", "tensor")
    paired = P("dp", None, "tensor")
    weights = (gain, flat, paired, flat, gain, paired, flat)
    shards = make_shards(mesh.shape["dp"])

    return jax.shard_map(
        shards,
        mesh=mesh,
        in_specs=(tokens, P("dp", None), tokens) + weights * 3,
        out_specs=(tokens, tokens) + weights * 4,
        check_vma=False,
    )
```

```python
import jax
import jax.numpy as jnp
from jax import lax
from jax.experimental import pallas as pl
from jax.experimental.pallas import tpu as pltpu
from jax.experimental.layout import Layout, with_layout_constraint
from jax.sharding import PartitionSpec as P


HEAD_DIM = 64

eps_norm = 1e-05
lr_rate = 0.025
beta_one = 0.9
beta_two = 0.999
adam_eps = 1e-08
decay_rate = 0.1
step_count = 2


def rows_major(values):
    return with_layout_constraint(values, Layout(major_to_minor=(0, 1)))


def ring_order(dp_size):
    if dp_size % 2:
        return list(range(dp_size))
    chips = dp_size // 2
    width = 2 if chips <= 8 else 4
    if chips % width:
        return list(range(dp_size))
    rows = chips // width
    ring = [row * width for row in range(rows)]
    for at, row in enumerate(reversed(range(rows))):
        columns = range(1, width) if at % 2 == 0 else reversed(range(1, width))
        ring += [row * width + column for column in columns]
    return [2 * chip + core for core in range(2) for chip in ring]


def permute_blocks(values, order):
    size = values.shape[-1] // len(order)
    if size % 128:
        parts = [values[..., o * size : (o + 1) * size] for o in order]
        return jnp.concatenate(parts, axis=-1)

    def body(values_ref, out_ref):
        for at, o in enumerate(order):
            out_ref[:, at * size : (at + 1) * size] = values_ref[:, o * size : (o + 1) * size]

    rows = values.shape[0] // 4
    spec = pl.BlockSpec((rows, values.shape[1]), lambda i: (i, 0))
    return pl.pallas_call(
        body,
        grid=(4,),
        in_specs=[spec],
        out_specs=spec,
        out_shape=jax.ShapeDtypeStruct(values.shape, values.dtype),
        cost_estimate=pl.CostEstimate(
            flops=0, transcendentals=0, bytes_accessed=2 * values.size * values.dtype.itemsize
        ),
    )(values)


def norm_parts(block_rows):
    inverse = lax.rsqrt(jnp.mean(block_rows * block_rows, axis=-1, keepdims=True) + eps_norm)
    return (block_rows * inverse, inverse)


def norm_back(grad_normed, gain_value, normed, inverse):
    scaled = grad_normed * gain_value
    return inverse * (scaled - normed * jnp.mean(scaled * normed, axis=-1, keepdims=True))


def rotary_tables(segments, head_width, first):
    earlier = jnp.sum((segments[None, :] < segments[:, None]).astype(jnp.int32), axis=1)
    position = jnp.arange(segments.shape[0], dtype=jnp.int32) - earlier
    half = segments.shape[0] // 2
    position = jnp.where(first == 0, position, jnp.concatenate([position[half:], position[:half]]))
    half_width = head_width // 2
    frequency = jnp.exp(
        jnp.arange(half_width, dtype=jnp.float32) * (-2.0 * jnp.log(10000.0) / head_width)
    )
    angles = position.astype(jnp.float32)[:, None] * frequency[None, :]
    angles = jnp.concatenate([angles] * 4, axis=1)
    return (jnp.cos(angles), jnp.sin(angles))


def nt_dot(left, right):
    return lax.dot_general(
        left, right, (((1,), (1,)), ((), ())), preferred_element_type=jnp.float32
    )


def plain_dot(left, right):
    return jnp.dot(left, right, preferred_element_type=jnp.float32)


def key_span(block):
    return max(0, block - 2), block + 1


def pair_mask(seg_column, seg_row, first, last, block, size):
    shape = ((last - first) * size, size)
    keys = lax.broadcasted_iota(jnp.int32, shape, 0) + first * size
    rows = lax.broadcasted_iota(jnp.int32, shape, 1) + block * size
    same = seg_column[first * size : last * size, :] == seg_row[:, block * size : (block + 1) * size]
    return same & (keys <= rows)


def both_sides(values, low):
    zero = jnp.zeros_like(values)
    left_first, right_second = jnp.where(low, values, zero), jnp.where(low, zero, values)
    return (
        (left_first, pltpu.roll(left_first, HEAD_DIM, 1)),
        (pltpu.roll(right_second, HEAD_DIM, 1), right_second),
    )


def attend_body(
    at_ref,
    qkv_ref,
    cos_ref,
    sin_ref,
    seg_column_ref,
    seg_row_ref,
    out_ref,
    query_ref,
    side_ref,
    key_ref,
    value_ref,
    log_ref,
    value_turned,
):
    bf16, f32 = jnp.bfloat16, jnp.float32
    seq_len, wide = out_ref.shape
    size, twice = seq_len // 4, 2 * HEAD_DIM
    half = HEAD_DIM // 2
    pairs = wide // twice
    scale = HEAD_DIM ** (-0.5)
    at = at_ref[0]
    lane = lax.broadcasted_iota(jnp.int32, (1, twice), 1)
    low, front = lane < HEAD_DIM, lane % HEAD_DIM < half

    def place(block):
        return pl.ds(pl.multiple_of((block + 2 * at) % 4 * size, size), size)

    def turned(values, rows):
        back = pltpu.roll(values, twice - half, 1)
        ahead = pltpu.roll(values, half, 1)
        return values * cos_ref[rows, :] + jnp.where(front, -back, ahead) * sin_ref[rows, :]

    for block in range(4):
        rows, natural = place(block), slice(block * size, (block + 1) * size)
        keys = turned(qkv_ref[rows, wide : wide + twice], rows).astype(bf16)
        values = qkv_ref[rows, wide + twice : wide + 2 * twice].astype(bf16)
        key_ref[natural, :] = keys
        value_ref[natural, :] = values
        for group, sides in enumerate(both_sides(keys.astype(f32), low)):
            for side in range(2):
                side_ref[group, side, natural, :] = sides[side].astype(bf16)
        value_turned[:, natural] = values.astype(f32).T.astype(bf16)

    def pair_step(pair, carry):
        lanes = pl.ds(pl.multiple_of(pair * twice, twice), twice)
        group = pair // (pairs // 2)
        for block in range(4):
            first, last = key_span(block)
            span = slice(first * size, last * size)
            rows = place(block)
            queries = turned(qkv_ref[rows, lanes], rows).astype(bf16)
            query_ref[rows, lanes] = queries
            mask = pair_mask(seg_column_ref, seg_row_ref, first, last, block, size)
            soft = []
            for side in range(2):
                scores = nt_dot(side_ref[group, side, span, :], queries) * scale
                scores = jnp.where(mask, scores, -1e30)
                top = jnp.max(scores, axis=0, keepdims=True)
                powers = jnp.exp(scores - top)
                total = jnp.sum(powers, axis=0, keepdims=True)
                log_ref[pair, side : side + 1, block * size : (block + 1) * size] = top + jnp.log(total)
                soft.append((powers * (1.0 / total)).astype(bf16))
            weights = value_turned[pl.ds(pl.multiple_of(group * HEAD_DIM, HEAD_DIM), HEAD_DIM), span]
            result = plain_dot(weights, jnp.concatenate(soft, axis=1))
            result = jnp.concatenate([result[:, :size], result[:, size:]], axis=0)
            out_ref[rows, lanes] = result.T.astype(bf16)
        return carry

    lax.fori_loop(0, pairs, pair_step, 0)


def attend_back_body(
    at_ref,
    grad_ref,
    query_ref,
    side_ref,
    key_ref,
    value_ref,
    log_ref,
    cos_ref,
    sin_ref,
    cos_turned_ref,
    sin_turned_ref,
    seg_column_ref,
    seg_row_ref,
    out_ref,
    value_side,
    key_turned,
    key_total,
    value_total,
):
    bf16, f32 = jnp.bfloat16, jnp.float32
    seq_len, wide = query_ref.shape
    size, twice = seq_len // 4, 2 * HEAD_DIM
    half = HEAD_DIM // 2
    pairs = wide // twice
    scale = HEAD_DIM ** (-0.5)
    at = at_ref[0]
    lane = lax.broadcasted_iota(jnp.int32, (1, twice), 1)
    low, front = lane < HEAD_DIM, lane % HEAD_DIM < half

    def place(block):
        return pl.ds(pl.multiple_of((block + 2 * at) % 4 * size, size), size)

    for block in range(4):
        natural = slice(block * size, (block + 1) * size)
        for group, sides in enumerate(both_sides(value_ref[natural, :].astype(f32), low)):
            for side in range(2):
                value_side[group, side, natural, :] = sides[side].astype(bf16)
        key_turned[:, natural] = key_ref[natural, :].astype(f32).T.astype(bf16)
    key_total[...] = jnp.zeros_like(key_total)
    value_total[...] = jnp.zeros_like(value_total)

    def split(values):
        zero = jnp.zeros_like(values)
        return jnp.concatenate([jnp.where(low, values, zero), jnp.where(low, zero, values)], axis=0)

    def pair_step(pair, carry):
        lanes = pl.ds(pl.multiple_of(pair * twice, twice), twice)
        group = pair // (pairs // 2)
        for block in range(4):
            first, last = key_span(block)
            span = slice(first * size, last * size)
            rows = place(block)
            queries, grads = query_ref[rows, lanes], grad_ref[rows, lanes]
            mask = pair_mask(seg_column_ref, seg_row_ref, first, last, block, size)
            soft, slopes = [], []
            for side in range(2):
                scores = nt_dot(side_ref[group, side, span, :], queries) * scale
                logs = log_ref[pair, side : side + 1, block * size : (block + 1) * size]
                weights = jnp.exp(jnp.where(mask, scores, -1e30) - logs)
                grad_soft = nt_dot(value_side[group, side, span, :], grads)
                delta = jnp.sum(weights * grad_soft, axis=0, keepdims=True)
                slopes.append((weights * (grad_soft - delta)).astype(bf16))
                soft.append(weights.astype(bf16))
            slopes, soft = jnp.concatenate(slopes, axis=1), jnp.concatenate(soft, axis=1)
            key_total[group, span, :] += plain_dot(slopes, split(queries))
            value_total[group, span, :] += plain_dot(soft, split(grads))
            keys = key_turned[pl.ds(pl.multiple_of(group * HEAD_DIM, HEAD_DIM), HEAD_DIM), span]
            result = plain_dot(keys, slopes) * scale
            cosine, sine = cos_turned_ref[:, rows], sin_turned_ref[:, rows]
            parts = []
            for side in range(2):
                own = result[:, side * size : (side + 1) * size]
                turn = own * sine
                own = own * cosine
                parts += [own[:half] + turn[half:], own[half:] - turn[:half]]
            out_ref[rows, lanes] = jnp.concatenate(parts, axis=0).T.astype(bf16)
        return carry

    lax.fori_loop(0, pairs, pair_step, 0)

    for block in range(4):
        rows, natural = place(block), slice(block * size, (block + 1) * size)
        folded = []
        for total in (key_total, value_total):
            groups = [total[group, natural, :] for group in range(2)]
            groups = [part + pltpu.roll(part, HEAD_DIM, 1) for part in groups]
            folded.append(jnp.where(low, groups[0], groups[1]))
        keys = folded[0] * scale
        turn = keys * sin_ref[rows, :]
        back, ahead = pltpu.roll(turn, twice - half, 1), pltpu.roll(turn, half, 1)
        keys = keys * cos_ref[rows, :] + jnp.where(front, back, -ahead)
        out_ref[rows, wide : wide + twice] = keys.astype(bf16)
        out_ref[rows, wide + twice : wide + 2 * twice] = folded[1].astype(bf16)


def whole_specs(count):
    return [pl.BlockSpec(memory_space=pltpu.SMEM)] + [pl.BlockSpec(memory_space=pltpu.VMEM)] * count


def attend(tensor_at, qkv, cosine, sine, segments, heads_wide):
    seq_len, bf16, f32 = qkv.shape[0], jnp.bfloat16, jnp.float32
    twice = 2 * HEAD_DIM
    shapes = (
        ((seq_len, heads_wide), bf16),
        ((seq_len, heads_wide), bf16),
        ((2, 2, seq_len, twice), bf16),
        ((seq_len, twice), bf16),
        ((seq_len, twice), bf16),
        ((heads_wide // twice, 2, seq_len), f32),
    )
    work = heads_wide * seq_len * seq_len
    return pl.pallas_call(
        attend_body,
        in_specs=whole_specs(5),
        out_specs=[pl.BlockSpec(memory_space=pltpu.VMEM)] * len(shapes),
        out_shape=[jax.ShapeDtypeStruct(shape, kind) for shape, kind in shapes],
        scratch_shapes=[pltpu.VMEM((twice, seq_len), bf16)],
        cost_estimate=pl.CostEstimate(
            flops=4 * work, transcendentals=work // HEAD_DIM, bytes_accessed=8 * qkv.size
        ),
    )(tensor_at[None], qkv, cosine, sine, segments[:, None], segments[None, :])


def attend_back(tensor_at, grad_cat, saved, cosine, sine, segments):
    queries, sides, keys, values, logs = saved
    (seq_len, heads_wide), bf16, f32 = queries.shape, jnp.bfloat16, jnp.float32
    twice = 2 * HEAD_DIM
    work = heads_wide * seq_len * seq_len
    return pl.pallas_call(
        attend_back_body,
        in_specs=whole_specs(12),
        out_specs=pl.BlockSpec(memory_space=pltpu.VMEM),
        out_shape=jax.ShapeDtypeStruct((seq_len, heads_wide + 2 * twice), bf16),
        scratch_shapes=[
            pltpu.VMEM((2, 2, seq_len, twice), bf16),
            pltpu.VMEM((twice, seq_len), bf16),
            pltpu.VMEM((2, seq_len, twice), f32),
            pltpu.VMEM((2, seq_len, twice), f32),
        ],
        cost_estimate=pl.CostEstimate(
            flops=10 * work, transcendentals=work // HEAD_DIM, bytes_accessed=8 * queries.size
        ),
    )(
        tensor_at[None],
        grad_cat,
        queries,
        sides,
        keys,
        values,
        logs,
        cosine,
        sine,
        cosine[:, :HEAD_DIM].T,
        sine[:, :HEAD_DIM].T,
        segments[:, None],
        segments[None, :],
    )


def cost_of(flops, *arrays):
    moved = sum(array.size * jnp.dtype(array.dtype).itemsize for array in arrays)
    return pl.CostEstimate(flops=flops, transcendentals=0, bytes_accessed=moved)


def tile_of(columns, most=256):
    return next(size for size in range(most, 0, -128) if columns % size == 0)


def by_rows(rows, step, chunk=256):
    chunk = min(chunk, rows)

    def one(at, carry):
        step(pl.ds(pl.multiple_of(at * chunk, chunk), chunk))
        return carry

    lax.fori_loop(0, rows // chunk, one, 0)


def times(left, right, first, columns, kind):
    rows, depth = left.shape
    tile = tile_of(columns)
    shape = jax.ShapeDtypeStruct((rows, columns), kind)

    def body(left_ref, right_ref, out_ref):
        def step(at):
            out_ref[at, :] = plain_dot(left_ref[at, :], right_ref[...]).astype(out_ref.dtype)

        by_rows(rows, step)

    return pl.pallas_call(
        body,
        grid=(columns // tile,),
        in_specs=[
            pl.BlockSpec((rows, depth), lambda j: (0, 0)),
            pl.BlockSpec((depth, tile), lambda j: (0, j + first // tile)),
        ],
        out_specs=pl.BlockSpec((rows, tile), lambda j: (0, j)),
        out_shape=shape,
        cost_estimate=cost_of(2 * rows * depth * columns, left, shape),
    )(left, right)


def times_turned(left, at, right, first, kind):
    stack = left if left.ndim == 3 else left[None]
    parts, rows, depth = stack.shape
    rows //= 2
    count, wide = right.shape
    tile = tile_of(count, 512)

    def body(left_ref, right_ref, out_ref):
        def step(rows_at):
            total = 0.0
            for part in range(parts):
                begin = first + part * depth
                total += nt_dot(left_ref[part, rows_at, :], right_ref[:, begin : begin + depth])
            out_ref[rows_at, :] = total.astype(out_ref.dtype)

        by_rows(rows, step)

    shape = jax.ShapeDtypeStruct((rows, count), kind)
    return pl.pallas_call(
        body,
        grid=(count // tile,),
        in_specs=[
            pl.BlockSpec((parts, rows, depth), lambda j: (0, at, 0)),
            pl.BlockSpec((tile, wide), lambda j: (j, 0)),
        ],
        out_specs=pl.BlockSpec((rows, tile), lambda j: (0, j)),
        out_shape=shape,
        cost_estimate=cost_of(2 * rows * depth * parts * count, right, shape),
    )(stack, right)


def turned_times(left, half, right, received=None):
    stack = right if right.ndim == 3 else right[None]
    parts, tokens, columns = stack.shape
    count = left.shape[1] // 2
    tile = tile_of(columns, max(512, columns // 2))
    tiles = columns // tile

    def body(half_ref, left_ref, right_ref, *rest):
        *received_ref, out_ref, turned = rest

        @pl.when(pl.program_id(0) == 0)
        def _():
            def turn(at, carry):
                columns_at = pl.ds(pl.multiple_of(at * 128, 128), 128)
                turned[columns_at, :] = left_ref[:, columns_at].astype(jnp.float32).T.astype(jnp.bfloat16)
                return carry

            lax.fori_loop(0, count // 128, turn, 0)

        def step(at):
            total = plain_dot(turned[at, :], right_ref[0])
            if received_ref:
                total += received_ref[0][at, :].astype(jnp.float32)
            out_ref[at, :] = total.astype(jnp.bfloat16)

        by_rows(count, step)

    block = pl.BlockSpec((count, tile), lambda j, half_ref: (0, j))
    shape = jax.ShapeDtypeStruct((count, parts * columns), jnp.bfloat16)
    more = [] if received is None else [received]
    return pl.pallas_call(
        body,
        grid_spec=pltpu.PrefetchScalarGridSpec(
            num_scalar_prefetch=1,
            grid=(parts * tiles,),
            in_specs=[
                pl.BlockSpec((tokens, count), lambda j, half_ref: (0, half_ref[0])),
                pl.BlockSpec((1, tokens, tile), lambda j, half_ref: (j // tiles, 0, j % tiles)),
            ]
            + [block] * len(more),
            out_specs=block,
            scratch_shapes=[pltpu.VMEM((count, tokens), jnp.bfloat16)],
        ),
        out_shape=shape,
        cost_estimate=cost_of(2 * tokens * count * parts * columns, stack, shape, *more),
    )(half[None], left, stack, *more)


def feed_forward(hidden, gate_up_all):
    rows, depth = hidden.shape
    wide = gate_up_all.shape[1] // 2
    tile = tile_of(wide)

    def body(hidden_ref, gate_ref, up_ref, gate_out, up_out, active_out):
        def step(at):
            gate_part = plain_dot(hidden_ref[at, :], gate_ref[...])
            upward = plain_dot(hidden_ref[at, :], up_ref[...])
            gate_out[at, :] = gate_part
            up_out[at, :] = upward
            active_out[at, :] = (gate_part * jax.nn.sigmoid(gate_part) * upward).astype(jnp.bfloat16)

        by_rows(rows, step)

    block = pl.BlockSpec((rows, tile), lambda j: (0, j))
    kinds = (jnp.float32, jnp.float32, jnp.bfloat16)
    shapes = [jax.ShapeDtypeStruct((rows, wide), kind) for kind in kinds]
    return pl.pallas_call(
        body,
        grid=(wide // tile,),
        in_specs=[
            pl.BlockSpec((rows, depth), lambda j: (0, 0)),
            pl.BlockSpec((depth, tile), lambda j: (0, j)),
            pl.BlockSpec((depth, tile), lambda j: (0, j + wide // tile)),
        ],
        out_specs=[block] * 3,
        out_shape=shapes,
        cost_estimate=cost_of(4 * rows * depth * wide, gate_up_all, *shapes),
    )(hidden, gate_up_all, gate_up_all)


def feed_forward_back(cot, down_all, gate_part, upward):
    rows, depth = cot.shape
    wide = down_all.shape[1]
    tile = tile_of(wide, wide // 2)

    def body(cot_ref, down_ref, gate_ref, up_ref, out_ref):
        def step(at):
            grad_act = plain_dot(cot_ref[at, :], down_ref[...])
            gate = gate_ref[at, :]
            sigmoid_gate = jax.nn.sigmoid(gate)
            slope = sigmoid_gate * (1.0 + gate * (1.0 - sigmoid_gate))
            out_ref[0, at, :] = (grad_act * up_ref[at, :] * slope).astype(jnp.bfloat16)
            out_ref[1, at, :] = (grad_act * (gate * sigmoid_gate)).astype(jnp.bfloat16)

        by_rows(rows, step)

    block = pl.BlockSpec((rows, tile), lambda j: (0, j))
    shape = jax.ShapeDtypeStruct((2, rows, wide), jnp.bfloat16)
    return pl.pallas_call(
        body,
        grid=(wide // tile,),
        in_specs=[
            pl.BlockSpec((rows, depth), lambda j: (0, 0)),
            pl.BlockSpec((depth, tile), lambda j: (0, j)),
            block,
            block,
        ],
        out_specs=pl.BlockSpec((2, rows, tile), lambda j: (0, 0, j)),
        out_shape=shape,
        cost_estimate=cost_of(2 * rows * depth * wide, down_all, gate_part, upward, shape),
    )(cot, down_all, gate_part, upward)


def adam_step(parameter, gradient, first_moment, second_moment):
    new_first = beta_one * first_moment + (1.0 - beta_one) * gradient
    new_second = beta_two * second_moment + (1.0 - beta_two) * gradient * gradient
    corrected_first = new_first / (1.0 - beta_one**step_count)
    corrected_second = new_second / (1.0 - beta_two**step_count)
    new_parameter = parameter - lr_rate * (
        corrected_first / (jnp.sqrt(corrected_second) + adam_eps) + decay_rate * parameter
    )
    return (new_parameter, new_first, new_second)


def pack(*weights):
    rows = weights[0].shape[0]
    wide = sum(weight.size // rows for weight in weights)

    def body(*refs):
        *weight_refs, out_ref = refs
        begin = 0
        for ref in weight_refs:
            for part in range(ref.shape[1]) if len(ref.shape) == 3 else (None,):
                values = ref[...] if part is None else ref[:, part, :]
                out_ref[:, begin : begin + ref.shape[-1]] = values.astype(jnp.bfloat16)
                begin += ref.shape[-1]

    shape = jax.ShapeDtypeStruct((rows, wide), jnp.bfloat16)
    return pl.pallas_call(
        body,
        in_specs=[pl.BlockSpec(memory_space=pltpu.VMEM)] * len(weights),
        out_specs=pl.BlockSpec(memory_space=pltpu.VMEM),
        out_shape=shape,
        cost_estimate=cost_of(shape.size, shape, *weights),
    )(*weights)


def adam_update(gradient, parameters, firsts, seconds, chunk):
    rows = gradient.shape[0]
    chunk = min(rows, chunk)
    count = len(parameters)

    def body(gradient_ref, *refs):
        old, new = refs[: 3 * count], refs[3 * count :]
        begin = 0
        for at in range(count):
            shape = old[3 * at].shape
            middle = range(shape[1]) if len(shape) == 3 else (None,)
            for part in middle:
                wide = shape[-1]
                where = (slice(None), slice(None)) if part is None else (slice(None), part, slice(None))
                grads = gradient_ref[:, begin : begin + wide].astype(jnp.float32)
                begin += wide
                results = adam_step(
                    old[3 * at][where], grads, old[3 * at + 1][where], old[3 * at + 2][where]
                )
                new[4 * at][where] = grads
                for index, result in enumerate(results):
                    new[4 * at + 1 + index][where] = result

    def spec(array):
        return pl.BlockSpec(
            (chunk,) + array.shape[1:], lambda i, zeros=(0,) * (array.ndim - 1): (i,) + zeros
        )

    inputs = [array for group in zip(parameters, firsts, seconds) for array in group]
    outputs = [array for array in parameters for _ in range(4)]
    results = pl.pallas_call(
        body,
        grid=(rows // chunk,),
        in_specs=[spec(gradient)] + [spec(array) for array in inputs],
        out_specs=[spec(array) for array in outputs],
        out_shape=[jax.ShapeDtypeStruct(array.shape, jnp.float32) for array in outputs],
        cost_estimate=cost_of(20 * gradient.size, *inputs, *outputs),
    )(gradient, *inputs)
    return [results[4 * at : 4 * at + 4] for at in range(count)]


def make_shards(dp_size):
    order = ring_order(dp_size)
    inverse_order = [order.index(i) for i in range(dp_size)]
    chips = dp_size // 2
    rings = [order[:chips], order[chips:]]

    def gather(values):
        return lax.all_gather(values, "dp", axis=0, tiled=True, axis_index_groups=[order])

    def scatter(values):
        return lax.psum_scatter(
            values, "dp", scatter_dimension=0, tiled=True, axis_index_groups=rings
        )

    def swap_core(values):
        return lax.ppermute(values, "dp", [(i, i ^ 1) for i in range(dp_size)])

    def pair_grad(left, right):
        core = lax.axis_index("dp") % 2
        other = turned_times(left, 1 - core, right)
        received = swap_core(other)
        return turned_times(left, core, right, received)

    def swap(values):
        return lax.ppermute(values, "tensor", [(0, 1), (1, 0)])

    def gather_small(values):
        at = lax.axis_index("dp")
        place = jnp.asarray(inverse_order, jnp.int32)[at]
        slots = lax.broadcasted_iota(jnp.int32, (1, dp_size, 1), 1) == place
        total = jnp.where(slots, values[:, None, :], jnp.zeros((), values.dtype))
        step = 1
        while step < dp_size:
            total = total + lax.ppermute(total, "dp", [(i, i ^ step) for i in range(dp_size)])
            step *= 2
        return total.reshape(values.shape[0], -1)

    def shards(
        block_input,
        segment_ids,
        cotangent,
        attn_gain,
        query_weight,
        key_value_weight,
        out_weight,
        feed_gain,
        gate_up_weight,
        down_weight,
        *moments,
    ):
        bf16, f32 = jnp.bfloat16, jnp.float32
        rows = attn_gain.shape[0]
        own = block_input.shape[0]
        heads_wide = query_weight.shape[1]
        keys_wide = key_value_weight.shape[2]
        tensor_at = lax.axis_index("tensor")

        qkv_wide = heads_wide + 2 * keys_wide
        gains = gather_small(jnp.stack([attn_gain, feed_gain]).astype(bf16)).astype(f32)
        attn_all = gather(pack(query_weight, key_value_weight, out_weight))
        gate_up_all = gather(gate_up_weight.astype(bf16).reshape(rows, -1))
        down_all = gather(down_weight.astype(bf16))
        gain_one, gain_two = gains[0:1], gains[1:2]

        block_rows = permute_blocks(block_input, order)
        cot_own = permute_blocks(cotangent, order)
        segments = segment_ids[0]
        cosine_table, sine_table = rotary_tables(segments, HEAD_DIM, tensor_at * own)

        def both(values):
            return jnp.concatenate([values, swap(values)], axis=0)

        def summed(left, right, first):
            partial = times_turned(left, 1, right, first, bf16)
            theirs = swap(partial)
            mine = times_turned(left, 0, right, first, f32)
            return mine + theirs.astype(f32)

        normed_one, inverse_one = norm_parts(block_rows)
        hidden_one = both((normed_one * gain_one).astype(bf16))
        cot_rows = both(cot_own.astype(bf16))

        qkv = times(hidden_one, attn_all, 0, qkv_wide, f32)
        attn_cat, *saved = attend(
            tensor_at, qkv, cosine_table, sine_table, segments, heads_wide
        )

        residual = block_rows + summed(attn_cat, attn_all, qkv_wide)
        normed_two, inverse_two = norm_parts(residual)
        hidden_two = both((normed_two * gain_two).astype(bf16))
        gate_part, upward, activated = feed_forward(hidden_two, gate_up_all)
        down_grad = pair_grad(cot_rows, activated)
        down_grad, down_all = lax.optimization_barrier((down_grad, down_all))
        down_sum = scatter(down_grad)
        grad_gate_up = feed_forward_back(cot_rows, down_all, gate_part, upward)
        grad_hidden_two = summed(grad_gate_up, gate_up_all, 0)
        gate_up_grad = pair_grad(hidden_two, grad_gate_up)
        gate_up_sum = scatter(gate_up_grad)
        feed_sum = summed(activated, down_all, 0)
        block_output = lax.optimization_barrier(residual) + feed_sum
        grad_residual = cot_own + norm_back(grad_hidden_two, gain_two, normed_two, inverse_two)
        feed_gain_part = jnp.sum(grad_hidden_two * normed_two, axis=0)
        grad_rows = both(grad_residual.astype(bf16))
        out_grad = pair_grad(grad_rows, attn_cat)
        grad_cat = times(grad_rows, attn_all, qkv_wide, heads_wide, bf16)
        grad_qkv = attend_back(
            tensor_at, grad_cat, saved, cosine_table, sine_table, segments
        )
        grad_hidden_one = summed(grad_qkv, attn_all, 0)
        qkv_grad = pair_grad(hidden_one, grad_qkv)
        input_grad = grad_residual + norm_back(grad_hidden_one, gain_one, normed_one, inverse_one)
        attn_gain_part = jnp.sum(grad_hidden_one * normed_one, axis=0)

        parts = [rows_major(qkv_grad), rows_major(out_grad)]
        attn_sum = rows_major(scatter(jnp.concatenate(parts, axis=1)))
        gain_parts = jnp.stack([attn_gain_part, feed_gain_part])
        gain_parts = gain_parts + swap(gain_parts)
        step = 1
        while step < dp_size:
            pairs = [(i, i ^ step) for i in range(dp_size)]
            gain_parts = gain_parts + lax.ppermute(gain_parts, "dp", pairs)
            step *= 2
        place = jnp.asarray(inverse_order, jnp.int32)[lax.axis_index("dp")]
        gain_sums = lax.dynamic_slice(gain_parts, (0, place * rows), (2, rows))
        attn_gain_sum, feed_gain_sum = gain_sums[0], gain_sums[1]

        count = len(moments) // 2
        firsts, seconds = moments[:count], moments[count:]

        def update(gradient, parameters, places, chunk):
            results = adam_update(
                gradient,
                parameters,
                [firsts[at] for at in places],
                [seconds[at] for at in places],
                chunk,
            )
            return dict(zip(places, results))

        attn_parameters = (query_weight, key_value_weight, out_weight)
        results = update(down_sum, (down_weight,), (6,), 32)
        results |= update(gate_up_sum, (gate_up_weight,), (5,), 16)
        results |= update(attn_sum, attn_parameters, (1, 2, 3), 64)
        for at, parameter, gradient in (
            (0, attn_gain, attn_gain_sum),
            (4, feed_gain, feed_gain_sum),
        ):
            results[at] = (gradient, *adam_step(parameter, gradient, firsts[at], seconds[at]))
        return (
            permute_blocks(block_output, inverse_order),
            permute_blocks(input_grad, inverse_order),
        ) + tuple(results[at][kind] for kind in range(4) for at in range(count))

    return shards


def solution(mesh):
    tokens = P(("dp", "tensor"), None)
    gain = P("dp")
    flat = P("dp", "tensor")
    paired = P("dp", None, "tensor")
    weights = (gain, flat, paired, flat, gain, paired, flat)
    shards = make_shards(mesh.shape["dp"])

    return jax.shard_map(
        shards,
        mesh=mesh,
        in_specs=(tokens, P("dp", None), tokens) + weights * 3,
        out_specs=(tokens, tokens) + weights * 4,
        check_vma=False,
    )
```

```python
import jax
import jax.numpy as jnp
from jax import lax
from jax.experimental import pallas as pl
from jax.experimental.pallas import tpu as pltpu
from jax.experimental.layout import Layout, with_layout_constraint
from jax.sharding import PartitionSpec as P


HEAD_DIM = 64

eps_norm = 1e-05
lr_rate = 0.025
beta_one = 0.9
beta_two = 0.999
adam_eps = 1e-08
decay_rate = 0.1
step_count = 2


def rows_major(values):
    return with_layout_constraint(values, Layout(major_to_minor=(0, 1)))


def ring_order(dp_size):
    if dp_size % 2:
        return list(range(dp_size))
    chips = dp_size // 2
    width = 2 if chips <= 8 else 4
    if chips % width:
        return list(range(dp_size))
    rows = chips // width
    ring = [row * width for row in range(rows)]
    for at, row in enumerate(reversed(range(rows))):
        columns = range(1, width) if at % 2 == 0 else reversed(range(1, width))
        ring += [row * width + column for column in columns]
    return [2 * chip + core for core in range(2) for chip in ring]


def permute_blocks(values, order):
    size = values.shape[-1] // len(order)
    if size % 128:
        parts = [values[..., o * size : (o + 1) * size] for o in order]
        return jnp.concatenate(parts, axis=-1)

    def body(values_ref, out_ref):
        for at, o in enumerate(order):
            out_ref[:, at * size : (at + 1) * size] = values_ref[:, o * size : (o + 1) * size]

    rows = values.shape[0] // 4
    spec = pl.BlockSpec((rows, values.shape[1]), lambda i: (i, 0))
    return pl.pallas_call(
        body,
        grid=(4,),
        in_specs=[spec],
        out_specs=spec,
        out_shape=jax.ShapeDtypeStruct(values.shape, values.dtype),
        cost_estimate=pl.CostEstimate(
            flops=0, transcendentals=0, bytes_accessed=2 * values.size * values.dtype.itemsize
        ),
    )(values)


def norm_parts(block_rows):
    inverse = lax.rsqrt(jnp.mean(block_rows * block_rows, axis=-1, keepdims=True) + eps_norm)
    return (block_rows * inverse, inverse)


def norm_back(grad_normed, gain_value, normed, inverse):
    scaled = grad_normed * gain_value
    return inverse * (scaled - normed * jnp.mean(scaled * normed, axis=-1, keepdims=True))


def rotary_tables(segments, head_width, first):
    earlier = jnp.sum((segments[None, :] < segments[:, None]).astype(jnp.int32), axis=1)
    position = jnp.arange(segments.shape[0], dtype=jnp.int32) - earlier
    half = segments.shape[0] // 2
    position = jnp.where(first == 0, position, jnp.concatenate([position[half:], position[:half]]))
    half_width = head_width // 2
    frequency = jnp.exp(
        jnp.arange(half_width, dtype=jnp.float32) * (-2.0 * jnp.log(10000.0) / head_width)
    )
    angles = position.astype(jnp.float32)[:, None] * frequency[None, :]
    angles = jnp.concatenate([angles] * 4, axis=1)
    return (jnp.cos(angles), jnp.sin(angles))


def nt_dot(left, right):
    return lax.dot_general(
        left, right, (((1,), (1,)), ((), ())), preferred_element_type=jnp.float32
    )


def plain_dot(left, right):
    return jnp.dot(left, right, preferred_element_type=jnp.float32)


def key_span(block):
    return max(0, block - 2), block + 1


def pair_mask(seg_column, seg_row, first, last, block, size):
    shape = ((last - first) * size, size)
    keys = lax.broadcasted_iota(jnp.int32, shape, 0) + first * size
    rows = lax.broadcasted_iota(jnp.int32, shape, 1) + block * size
    same = seg_column[first * size : last * size, :] == seg_row[:, block * size : (block + 1) * size]
    return same & (keys <= rows)


def both_sides(values, low):
    zero = jnp.zeros_like(values)
    left_first, right_second = jnp.where(low, values, zero), jnp.where(low, zero, values)
    return (
        (left_first, pltpu.roll(left_first, HEAD_DIM, 1)),
        (pltpu.roll(right_second, HEAD_DIM, 1), right_second),
    )


def attend_body(
    at_ref,
    qkv_ref,
    cos_ref,
    sin_ref,
    seg_column_ref,
    seg_row_ref,
    out_ref,
    query_ref,
    side_ref,
    key_ref,
    value_ref,
    log_ref,
    value_turned,
):
    bf16, f32 = jnp.bfloat16, jnp.float32
    seq_len, wide = out_ref.shape
    size, twice = seq_len // 4, 2 * HEAD_DIM
    half = HEAD_DIM // 2
    pairs = wide // twice
    scale = HEAD_DIM ** (-0.5)
    at = at_ref[0]
    lane = lax.broadcasted_iota(jnp.int32, (1, twice), 1)
    low, front = lane < HEAD_DIM, lane % HEAD_DIM < half

    def place(block):
        return pl.ds(pl.multiple_of((block + 2 * at) % 4 * size, size), size)

    def turned(values, rows):
        back = pltpu.roll(values, twice - half, 1)
        ahead = pltpu.roll(values, half, 1)
        return values * cos_ref[rows, :] + jnp.where(front, -back, ahead) * sin_ref[rows, :]

    for block in range(4):
        rows, natural = place(block), slice(block * size, (block + 1) * size)
        keys = turned(qkv_ref[rows, wide : wide + twice], rows).astype(bf16)
        values = qkv_ref[rows, wide + twice : wide + 2 * twice].astype(bf16)
        key_ref[natural, :] = keys
        value_ref[natural, :] = values
        for group, sides in enumerate(both_sides(keys.astype(f32), low)):
            for side in range(2):
                side_ref[group, side, natural, :] = sides[side].astype(bf16)
        value_turned[:, natural] = values.astype(f32).T.astype(bf16)

    def pair_step(pair, carry):
        lanes = pl.ds(pl.multiple_of(pair * twice, twice), twice)
        group = pair // (pairs // 2)
        for block in range(4):
            first, last = key_span(block)
            span = slice(first * size, last * size)
            rows = place(block)
            queries = turned(qkv_ref[rows, lanes], rows).astype(bf16)
            query_ref[rows, lanes] = queries
            mask = pair_mask(seg_column_ref, seg_row_ref, first, last, block, size)
            soft = []
            for side in range(2):
                scores = nt_dot(side_ref[group, side, span, :], queries) * scale
                scores = jnp.where(mask, scores, -1e30)
                top = jnp.max(scores, axis=0, keepdims=True)
                powers = jnp.exp(scores - top)
                total = jnp.sum(powers, axis=0, keepdims=True)
                log_ref[pair, side : side + 1, block * size : (block + 1) * size] = top + jnp.log(total)
                soft.append((powers * (1.0 / total)).astype(bf16))
            weights = value_turned[pl.ds(pl.multiple_of(group * HEAD_DIM, HEAD_DIM), HEAD_DIM), span]
            result = plain_dot(weights, jnp.concatenate(soft, axis=1))
            result = jnp.concatenate([result[:, :size], result[:, size:]], axis=0)
            out_ref[rows, lanes] = result.T.astype(bf16)
        return carry

    lax.fori_loop(0, pairs, pair_step, 0)


def attend_back_body(
    at_ref,
    grad_ref,
    query_ref,
    side_ref,
    key_ref,
    value_ref,
    log_ref,
    cos_ref,
    sin_ref,
    cos_turned_ref,
    sin_turned_ref,
    seg_column_ref,
    seg_row_ref,
    out_ref,
    value_side,
    key_turned,
    key_total,
    value_total,
):
    bf16, f32 = jnp.bfloat16, jnp.float32
    seq_len, wide = query_ref.shape
    size, twice = seq_len // 4, 2 * HEAD_DIM
    half = HEAD_DIM // 2
    pairs = wide // twice
    scale = HEAD_DIM ** (-0.5)
    at = at_ref[0]
    lane = lax.broadcasted_iota(jnp.int32, (1, twice), 1)
    low, front = lane < HEAD_DIM, lane % HEAD_DIM < half

    def place(block):
        return pl.ds(pl.multiple_of((block + 2 * at) % 4 * size, size), size)

    for block in range(4):
        natural = slice(block * size, (block + 1) * size)
        for group, sides in enumerate(both_sides(value_ref[natural, :].astype(f32), low)):
            for side in range(2):
                value_side[group, side, natural, :] = sides[side].astype(bf16)
        key_turned[:, natural] = key_ref[natural, :].astype(f32).T.astype(bf16)
    key_total[...] = jnp.zeros_like(key_total)
    value_total[...] = jnp.zeros_like(value_total)

    def split(values):
        zero = jnp.zeros_like(values)
        return jnp.concatenate([jnp.where(low, values, zero), jnp.where(low, zero, values)], axis=0)

    def pair_step(pair, carry):
        lanes = pl.ds(pl.multiple_of(pair * twice, twice), twice)
        group = pair // (pairs // 2)
        for block in range(4):
            first, last = key_span(block)
            span = slice(first * size, last * size)
            rows = place(block)
            queries, grads = query_ref[rows, lanes], grad_ref[rows, lanes]
            mask = pair_mask(seg_column_ref, seg_row_ref, first, last, block, size)
            soft, slopes = [], []
            for side in range(2):
                scores = nt_dot(side_ref[group, side, span, :], queries) * scale
                logs = log_ref[pair, side : side + 1, block * size : (block + 1) * size]
                weights = jnp.exp(jnp.where(mask, scores, -1e30) - logs)
                grad_soft = nt_dot(value_side[group, side, span, :], grads)
                delta = jnp.sum(weights * grad_soft, axis=0, keepdims=True)
                slopes.append((weights * (grad_soft - delta)).astype(bf16))
                soft.append(weights.astype(bf16))
            slopes, soft = jnp.concatenate(slopes, axis=1), jnp.concatenate(soft, axis=1)
            key_total[group, span, :] += plain_dot(slopes, split(queries))
            value_total[group, span, :] += plain_dot(soft, split(grads))
            keys = key_turned[pl.ds(pl.multiple_of(group * HEAD_DIM, HEAD_DIM), HEAD_DIM), span]
            result = plain_dot(keys, slopes) * scale
            cosine, sine = cos_turned_ref[:, rows], sin_turned_ref[:, rows]
            parts = []
            for side in range(2):
                own = result[:, side * size : (side + 1) * size]
                turn = own * sine
                own = own * cosine
                parts += [own[:half] + turn[half:], own[half:] - turn[:half]]
            out_ref[rows, lanes] = jnp.concatenate(parts, axis=0).T.astype(bf16)
        return carry

    lax.fori_loop(0, pairs, pair_step, 0)

    for block in range(4):
        rows, natural = place(block), slice(block * size, (block + 1) * size)
        folded = []
        for total in (key_total, value_total):
            groups = [total[group, natural, :] for group in range(2)]
            groups = [part + pltpu.roll(part, HEAD_DIM, 1) for part in groups]
            folded.append(jnp.where(low, groups[0], groups[1]))
        keys = folded[0] * scale
        turn = keys * sin_ref[rows, :]
        back, ahead = pltpu.roll(turn, twice - half, 1), pltpu.roll(turn, half, 1)
        keys = keys * cos_ref[rows, :] + jnp.where(front, back, -ahead)
        out_ref[rows, wide : wide + twice] = keys.astype(bf16)
        out_ref[rows, wide + twice : wide + 2 * twice] = folded[1].astype(bf16)


def whole_specs(count):
    return [pl.BlockSpec(memory_space=pltpu.SMEM)] + [pl.BlockSpec(memory_space=pltpu.VMEM)] * count


def attend(tensor_at, qkv, cosine, sine, segments, heads_wide):
    seq_len, bf16, f32 = qkv.shape[0], jnp.bfloat16, jnp.float32
    twice = 2 * HEAD_DIM
    shapes = (
        ((seq_len, heads_wide), bf16),
        ((seq_len, heads_wide), bf16),
        ((2, 2, seq_len, twice), bf16),
        ((seq_len, twice), bf16),
        ((seq_len, twice), bf16),
        ((heads_wide // twice, 2, seq_len), f32),
    )
    work = heads_wide * seq_len * seq_len
    return pl.pallas_call(
        attend_body,
        in_specs=whole_specs(5),
        out_specs=[pl.BlockSpec(memory_space=pltpu.VMEM)] * len(shapes),
        out_shape=[jax.ShapeDtypeStruct(shape, kind) for shape, kind in shapes],
        scratch_shapes=[pltpu.VMEM((twice, seq_len), bf16)],
        cost_estimate=pl.CostEstimate(
            flops=4 * work, transcendentals=work // HEAD_DIM, bytes_accessed=8 * qkv.size
        ),
    )(tensor_at[None], qkv, cosine, sine, segments[:, None], segments[None, :])


def attend_back(tensor_at, grad_cat, saved, cosine, sine, segments):
    queries, sides, keys, values, logs = saved
    (seq_len, heads_wide), bf16, f32 = queries.shape, jnp.bfloat16, jnp.float32
    twice = 2 * HEAD_DIM
    work = heads_wide * seq_len * seq_len
    return pl.pallas_call(
        attend_back_body,
        in_specs=whole_specs(12),
        out_specs=pl.BlockSpec(memory_space=pltpu.VMEM),
        out_shape=jax.ShapeDtypeStruct((seq_len, heads_wide + 2 * twice), bf16),
        scratch_shapes=[
            pltpu.VMEM((2, 2, seq_len, twice), bf16),
            pltpu.VMEM((twice, seq_len), bf16),
            pltpu.VMEM((2, seq_len, twice), f32),
            pltpu.VMEM((2, seq_len, twice), f32),
        ],
        cost_estimate=pl.CostEstimate(
            flops=10 * work, transcendentals=work // HEAD_DIM, bytes_accessed=8 * queries.size
        ),
    )(
        tensor_at[None],
        grad_cat,
        queries,
        sides,
        keys,
        values,
        logs,
        cosine,
        sine,
        cosine[:, :HEAD_DIM].T,
        sine[:, :HEAD_DIM].T,
        segments[:, None],
        segments[None, :],
    )


def cost_of(flops, *arrays):
    moved = sum(array.size * jnp.dtype(array.dtype).itemsize for array in arrays)
    return pl.CostEstimate(flops=flops, transcendentals=0, bytes_accessed=moved)


def tile_of(columns, most=256):
    return next(size for size in range(most, 0, -128) if columns % size == 0)


def by_rows(rows, step, chunk=256):
    chunk = min(chunk, rows)

    def one(at, carry):
        step(pl.ds(pl.multiple_of(at * chunk, chunk), chunk))
        return carry

    lax.fori_loop(0, rows // chunk, one, 0)


def times(left, right, first, columns, kind):
    rows, depth = left.shape
    tile = tile_of(columns)
    shape = jax.ShapeDtypeStruct((rows, columns), kind)

    def body(left_ref, right_ref, out_ref):
        def step(at):
            out_ref[at, :] = plain_dot(left_ref[at, :], right_ref[...]).astype(out_ref.dtype)

        by_rows(rows, step)

    return pl.pallas_call(
        body,
        grid=(columns // tile,),
        in_specs=[
            pl.BlockSpec((rows, depth), lambda j: (0, 0)),
            pl.BlockSpec((depth, tile), lambda j: (0, j + first // tile)),
        ],
        out_specs=pl.BlockSpec((rows, tile), lambda j: (0, j)),
        out_shape=shape,
        cost_estimate=cost_of(2 * rows * depth * columns, left, shape),
    )(left, right)


def times_turned(left, at, right, first, kind):
    stack = left if left.ndim == 3 else left[None]
    parts, rows, depth = stack.shape
    rows //= 2
    count, wide = right.shape
    tile = tile_of(count, 512)

    def body(left_ref, right_ref, out_ref):
        def step(rows_at):
            total = 0.0
            for part in range(parts):
                begin = first + part * depth
                total += nt_dot(left_ref[part, rows_at, :], right_ref[:, begin : begin + depth])
            out_ref[rows_at, :] = total.astype(out_ref.dtype)

        by_rows(rows, step)

    shape = jax.ShapeDtypeStruct((rows, count), kind)
    return pl.pallas_call(
        body,
        grid=(count // tile,),
        in_specs=[
            pl.BlockSpec((parts, rows, depth), lambda j: (0, at, 0)),
            pl.BlockSpec((tile, wide), lambda j: (j, 0)),
        ],
        out_specs=pl.BlockSpec((rows, tile), lambda j: (0, j)),
        out_shape=shape,
        cost_estimate=cost_of(2 * rows * depth * parts * count, right, shape),
    )(stack, right)


def turned_times(left, half, right, received=None):
    stack = right if right.ndim == 3 else right[None]
    parts, tokens, columns = stack.shape
    count = left.shape[1] // 2
    tile = tile_of(columns, max(512, columns // 2))
    tiles = columns // tile

    def body(half_ref, left_ref, right_ref, *rest):
        *received_ref, out_ref, turned = rest

        @pl.when(pl.program_id(0) == 0)
        def _():
            def turn(at, carry):
                columns_at = pl.ds(pl.multiple_of(at * 128, 128), 128)
                turned[columns_at, :] = left_ref[:, columns_at].astype(jnp.float32).T.astype(jnp.bfloat16)
                return carry

            lax.fori_loop(0, count // 128, turn, 0)

        def step(at):
            total = plain_dot(turned[at, :], right_ref[0])
            if received_ref:
                total += received_ref[0][at, :].astype(jnp.float32)
            out_ref[at, :] = total.astype(jnp.bfloat16)

        by_rows(count, step)

    block = pl.BlockSpec((count, tile), lambda j, half_ref: (0, j))
    shape = jax.ShapeDtypeStruct((count, parts * columns), jnp.bfloat16)
    more = [] if received is None else [received]
    return pl.pallas_call(
        body,
        grid_spec=pltpu.PrefetchScalarGridSpec(
            num_scalar_prefetch=1,
            grid=(parts * tiles,),
            in_specs=[
                pl.BlockSpec((tokens, count), lambda j, half_ref: (0, half_ref[0])),
                pl.BlockSpec((1, tokens, tile), lambda j, half_ref: (j // tiles, 0, j % tiles)),
            ]
            + [block] * len(more),
            out_specs=block,
            scratch_shapes=[pltpu.VMEM((count, tokens), jnp.bfloat16)],
        ),
        out_shape=shape,
        cost_estimate=cost_of(2 * tokens * count * parts * columns, stack, shape, *more),
    )(half[None], left, stack, *more)


def feed_forward(hidden, gate_up_all):
    rows, depth = hidden.shape
    wide = gate_up_all.shape[1] // 2
    tile = tile_of(wide)

    def body(hidden_ref, gate_ref, up_ref, gate_out, up_out, active_out):
        def step(at):
            gate_part = plain_dot(hidden_ref[at, :], gate_ref[...])
            upward = plain_dot(hidden_ref[at, :], up_ref[...])
            gate_out[at, :] = gate_part
            up_out[at, :] = upward
            active_out[at, :] = (gate_part * jax.nn.sigmoid(gate_part) * upward).astype(jnp.bfloat16)

        by_rows(rows, step)

    block = pl.BlockSpec((rows, tile), lambda j: (0, j))
    kinds = (jnp.float32, jnp.float32, jnp.bfloat16)
    shapes = [jax.ShapeDtypeStruct((rows, wide), kind) for kind in kinds]
    return pl.pallas_call(
        body,
        grid=(wide // tile,),
        in_specs=[
            pl.BlockSpec((rows, depth), lambda j: (0, 0)),
            pl.BlockSpec((depth, tile), lambda j: (0, j)),
            pl.BlockSpec((depth, tile), lambda j: (0, j + wide // tile)),
        ],
        out_specs=[block] * 3,
        out_shape=shapes,
        cost_estimate=cost_of(4 * rows * depth * wide, gate_up_all, *shapes),
    )(hidden, gate_up_all, gate_up_all)


def feed_forward_back(cot, down_all, gate_part, upward):
    rows, depth = cot.shape
    wide = down_all.shape[1]
    tile = tile_of(wide, wide // 2)

    def body(cot_ref, down_ref, gate_ref, up_ref, out_ref):
        def step(at):
            grad_act = plain_dot(cot_ref[at, :], down_ref[...])
            gate = gate_ref[at, :]
            sigmoid_gate = jax.nn.sigmoid(gate)
            slope = sigmoid_gate * (1.0 + gate * (1.0 - sigmoid_gate))
            out_ref[0, at, :] = (grad_act * up_ref[at, :] * slope).astype(jnp.bfloat16)
            out_ref[1, at, :] = (grad_act * (gate * sigmoid_gate)).astype(jnp.bfloat16)

        by_rows(rows, step)

    block = pl.BlockSpec((rows, tile), lambda j: (0, j))
    shape = jax.ShapeDtypeStruct((2, rows, wide), jnp.bfloat16)
    return pl.pallas_call(
        body,
        grid=(wide // tile,),
        in_specs=[
            pl.BlockSpec((rows, depth), lambda j: (0, 0)),
            pl.BlockSpec((depth, tile), lambda j: (0, j)),
            block,
            block,
        ],
        out_specs=pl.BlockSpec((2, rows, tile), lambda j: (0, 0, j)),
        out_shape=shape,
        cost_estimate=cost_of(2 * rows * depth * wide, down_all, gate_part, upward, shape),
    )(cot, down_all, gate_part, upward)


def adam_step(parameter, gradient, first_moment, second_moment):
    new_first = beta_one * first_moment + (1.0 - beta_one) * gradient
    new_second = beta_two * second_moment + (1.0 - beta_two) * gradient * gradient
    corrected_first = new_first / (1.0 - beta_one**step_count)
    corrected_second = new_second / (1.0 - beta_two**step_count)
    new_parameter = parameter - lr_rate * (
        corrected_first / (jnp.sqrt(corrected_second) + adam_eps) + decay_rate * parameter
    )
    return (new_parameter, new_first, new_second)


def pack(*weights):
    rows = weights[0].shape[0]
    wide = sum(weight.size // rows for weight in weights)

    def body(*refs):
        *weight_refs, out_ref = refs
        begin = 0
        for ref in weight_refs:
            for part in range(ref.shape[1]) if len(ref.shape) == 3 else (None,):
                values = ref[...] if part is None else ref[:, part, :]
                out_ref[:, begin : begin + ref.shape[-1]] = values.astype(jnp.bfloat16)
                begin += ref.shape[-1]

    shape = jax.ShapeDtypeStruct((rows, wide), jnp.bfloat16)
    blocks = 4

    def spec(array):
        inner = array.shape[1:]
        return pl.BlockSpec((rows // blocks,) + inner, lambda i: (i,) + (0,) * len(inner))

    return pl.pallas_call(
        body,
        grid=(blocks,),
        in_specs=[spec(weight) for weight in weights],
        out_specs=spec(shape),
        out_shape=shape,
        cost_estimate=cost_of(shape.size, shape, *weights),
    )(*weights)


def adam_update(gradient, parameters, firsts, seconds, chunk, resident):
    rows = gradient.shape[0]
    chunk = min(rows, chunk)
    count = len(parameters)

    def body(gradient_ref, *refs):
        old, new = refs[: 3 * count], refs[3 * count :]
        rows_at = pl.ds(pl.multiple_of(pl.program_id(0) * chunk, chunk), chunk)
        begin = 0
        for at in range(count):
            shape = old[3 * at].shape
            middle = range(shape[1]) if len(shape) == 3 else (None,)
            for part in middle:
                wide = shape[-1]
                middles = () if part is None else (part,)
                where = (slice(None), *middles, slice(None))
                source = (rows_at, *middles, slice(None)) if resident else where
                grads = gradient_ref[:, begin : begin + wide].astype(jnp.float32)
                begin += wide
                results = adam_step(
                    old[3 * at][source], grads, old[3 * at + 1][source], old[3 * at + 2][source]
                )
                new[4 * at][where] = grads
                for index, result in enumerate(results):
                    new[4 * at + 1 + index][where] = result

    def spec(array):
        return pl.BlockSpec(
            (chunk,) + array.shape[1:], lambda i, zeros=(0,) * (array.ndim - 1): (i,) + zeros
        )

    inputs = [array for group in zip(parameters, firsts, seconds) for array in group]
    if resident:
        inputs = [pltpu.with_memory_space_constraint(array, pltpu.VMEM) for array in inputs]
    outputs = [array for array in parameters for _ in range(4)]
    results = pl.pallas_call(
        body,
        grid=(rows // chunk,),
        in_specs=[spec(gradient)]
        + [
            pl.BlockSpec(memory_space=pltpu.VMEM) if resident else spec(array) for array in inputs
        ],
        out_specs=[spec(array) for array in outputs],
        out_shape=[jax.ShapeDtypeStruct(array.shape, jnp.float32) for array in outputs],
        cost_estimate=cost_of(20 * gradient.size, *inputs, *outputs),
    )(gradient, *inputs)
    return [results[4 * at : 4 * at + 4] for at in range(count)]


def make_shards(dp_size):
    order = ring_order(dp_size)
    inverse_order = [order.index(i) for i in range(dp_size)]
    chips = dp_size // 2
    rings = [order[:chips], order[chips:]]

    def gather(values):
        return lax.all_gather(values, "dp", axis=0, tiled=True, axis_index_groups=[order])

    def scatter(values):
        return lax.psum_scatter(
            values, "dp", scatter_dimension=0, tiled=True, axis_index_groups=rings
        )

    def swap_core(values):
        return lax.ppermute(values, "dp", [(i, i ^ 1) for i in range(dp_size)])

    def pair_grad(left, right):
        core = lax.axis_index("dp") % 2
        other = turned_times(left, 1 - core, right)
        received = swap_core(other)
        return turned_times(left, core, right, received)

    def swap(values):
        return lax.ppermute(values, "tensor", [(0, 1), (1, 0)])

    def gather_small(values):
        at = lax.axis_index("dp")
        place = jnp.asarray(inverse_order, jnp.int32)[at]
        slots = lax.broadcasted_iota(jnp.int32, (1, dp_size, 1), 1) == place
        total = jnp.where(slots, values[:, None, :], jnp.zeros((), values.dtype))
        step = 1
        while step < dp_size:
            total = total + lax.ppermute(total, "dp", [(i, i ^ step) for i in range(dp_size)])
            step *= 2
        return total.reshape(values.shape[0], -1)

    def shards(
        block_input,
        segment_ids,
        cotangent,
        attn_gain,
        query_weight,
        key_value_weight,
        out_weight,
        feed_gain,
        gate_up_weight,
        down_weight,
        *moments,
    ):
        bf16, f32 = jnp.bfloat16, jnp.float32
        rows = attn_gain.shape[0]
        own = block_input.shape[0]
        heads_wide = query_weight.shape[1]
        keys_wide = key_value_weight.shape[2]
        tensor_at = lax.axis_index("tensor")

        qkv_wide = heads_wide + 2 * keys_wide
        gains = gather_small(jnp.stack([attn_gain, feed_gain]).astype(bf16)).astype(f32)
        attn_all = gather(pack(query_weight, key_value_weight, out_weight))
        gate_up_all = gather(gate_up_weight.astype(bf16).reshape(rows, -1))
        down_all = gather(down_weight.astype(bf16))
        gain_one, gain_two = gains[0:1], gains[1:2]

        block_rows = permute_blocks(block_input, order)
        cot_own = permute_blocks(cotangent, order)
        segments = segment_ids[0]
        cosine_table, sine_table = rotary_tables(segments, HEAD_DIM, tensor_at * own)

        def both(values):
            return jnp.concatenate([values, swap(values)], axis=0)

        def summed(left, right, first):
            partial = times_turned(left, 1, right, first, bf16)
            theirs = swap(partial)
            mine = times_turned(left, 0, right, first, f32)
            return mine + theirs.astype(f32)

        normed_one, inverse_one = norm_parts(block_rows)
        hidden_one = both((normed_one * gain_one).astype(bf16))
        cot_rows = both(cot_own.astype(bf16))

        qkv = times(hidden_one, attn_all, 0, qkv_wide, f32)
        attn_cat, *saved = attend(tensor_at, qkv, cosine_table, sine_table, segments, heads_wide)

        residual = block_rows + summed(attn_cat, attn_all, qkv_wide)
        normed_two, inverse_two = norm_parts(residual)
        hidden_two = both((normed_two * gain_two).astype(bf16))
        gate_part, upward, activated = feed_forward(hidden_two, gate_up_all)
        down_grad = pair_grad(cot_rows, activated)
        down_grad, down_all = lax.optimization_barrier((down_grad, down_all))
        down_sum = scatter(down_grad)
        grad_gate_up = feed_forward_back(cot_rows, down_all, gate_part, upward)
        grad_hidden_two = summed(grad_gate_up, gate_up_all, 0)
        gate_up_grad = pair_grad(hidden_two, grad_gate_up)
        gate_up_sum = scatter(gate_up_grad)
        feed_sum = summed(activated, down_all, 0)
        block_output = lax.optimization_barrier(residual) + feed_sum
        grad_residual = cot_own + norm_back(grad_hidden_two, gain_two, normed_two, inverse_two)
        feed_gain_part = jnp.sum(grad_hidden_two * normed_two, axis=0)
        grad_rows = both(grad_residual.astype(bf16))
        out_grad = pair_grad(grad_rows, attn_cat)
        grad_cat = times(grad_rows, attn_all, qkv_wide, heads_wide, bf16)
        grad_qkv = attend_back(
            tensor_at, grad_cat, saved, cosine_table, sine_table, segments
        )
        grad_hidden_one = summed(grad_qkv, attn_all, 0)
        qkv_grad = pair_grad(hidden_one, grad_qkv)
        input_grad = grad_residual + norm_back(grad_hidden_one, gain_one, normed_one, inverse_one)
        attn_gain_part = jnp.sum(grad_hidden_one * normed_one, axis=0)

        parts = [rows_major(qkv_grad), rows_major(out_grad)]
        attn_sum = rows_major(scatter(jnp.concatenate(parts, axis=1)))
        gain_parts = jnp.stack([attn_gain_part, feed_gain_part])
        gain_parts = gain_parts + swap(gain_parts)
        step = 1
        while step < dp_size:
            pairs = [(i, i ^ step) for i in range(dp_size)]
            gain_parts = gain_parts + lax.ppermute(gain_parts, "dp", pairs)
            step *= 2
        place = jnp.asarray(inverse_order, jnp.int32)[lax.axis_index("dp")]
        gain_sums = lax.dynamic_slice(gain_parts, (0, place * rows), (2, rows))
        attn_gain_sum, feed_gain_sum = gain_sums[0], gain_sums[1]

        count = len(moments) // 2
        firsts, seconds = moments[:count], moments[count:]

        def update(gradient, parameters, places, chunk, resident=False):
            results = adam_update(
                gradient,
                parameters,
                [firsts[at] for at in places],
                [seconds[at] for at in places],
                chunk,
                resident,
            )
            return dict(zip(places, results))

        attn_parameters = (query_weight, key_value_weight, out_weight)
        results = update(down_sum, (down_weight,), (6,), 32)
        results |= update(gate_up_sum, (gate_up_weight,), (5,), 16)
        results |= update(attn_sum, attn_parameters, (1, 2, 3), 32, True)
        for at, parameter, gradient in (
            (0, attn_gain, attn_gain_sum),
            (4, feed_gain, feed_gain_sum),
        ):
            results[at] = (gradient, *adam_step(parameter, gradient, firsts[at], seconds[at]))
        return (
            permute_blocks(block_output, inverse_order),
            permute_blocks(input_grad, inverse_order),
        ) + tuple(results[at][kind] for kind in range(4) for at in range(count))

    return shards


def solution(mesh):
    tokens = P(("dp", "tensor"), None)
    gain = P("dp")
    flat = P("dp", "tensor")
    paired = P("dp", None, "tensor")
    weights = (gain, flat, paired, flat, gain, paired, flat)
    shards = make_shards(mesh.shape["dp"])

    return jax.shard_map(
        shards,
        mesh=mesh,
        in_specs=(tokens, P("dp", None), tokens) + weights * 3,
        out_specs=(tokens, tokens) + weights * 4,
        check_vma=False,
    )
```

```python
import jax
import jax.numpy as jnp
from jax import lax
from jax.experimental import pallas as pl
from jax.experimental.pallas import tpu as pltpu
from jax.experimental.layout import Layout, with_layout_constraint
from jax.sharding import PartitionSpec as P


HEAD_DIM = 64

eps_norm = 1e-05
lr_rate = 0.025
beta_one = 0.9
beta_two = 0.999
adam_eps = 1e-08
decay_rate = 0.1
step_count = 2


def rows_major(values):
    return with_layout_constraint(values, Layout(major_to_minor=(0, 1)))


def ring_order(dp_size):
    if dp_size % 2:
        return list(range(dp_size))
    chips = dp_size // 2
    width = 2 if chips <= 8 else 4
    if chips % width:
        return list(range(dp_size))
    rows = chips // width
    ring = [row * width for row in range(rows)]
    for at, row in enumerate(reversed(range(rows))):
        columns = range(1, width) if at % 2 == 0 else reversed(range(1, width))
        ring += [row * width + column for column in columns]
    return [2 * chip + core for core in range(2) for chip in ring]


def permute_blocks(values, order):
    size = values.shape[-1] // len(order)
    if size % 128:
        parts = [values[..., o * size : (o + 1) * size] for o in order]
        return jnp.concatenate(parts, axis=-1)

    def body(values_ref, out_ref):
        for at, o in enumerate(order):
            out_ref[:, at * size : (at + 1) * size] = values_ref[:, o * size : (o + 1) * size]

    rows = values.shape[0] // 4
    spec = pl.BlockSpec((rows, values.shape[1]), lambda i: (i, 0))
    return pl.pallas_call(
        body,
        grid=(4,),
        in_specs=[spec],
        out_specs=spec,
        out_shape=jax.ShapeDtypeStruct(values.shape, values.dtype),
        cost_estimate=pl.CostEstimate(
            flops=0, transcendentals=0, bytes_accessed=2 * values.size * values.dtype.itemsize
        ),
    )(values)


def norm_parts(block_rows):
    inverse = lax.rsqrt(jnp.mean(block_rows * block_rows, axis=-1, keepdims=True) + eps_norm)
    return (block_rows * inverse, inverse)


def norm_back(grad_normed, gain_value, normed, inverse):
    scaled = grad_normed * gain_value
    return inverse * (scaled - normed * jnp.mean(scaled * normed, axis=-1, keepdims=True))


def rotary_tables(segments, head_width, first):
    earlier = jnp.sum((segments[None, :] < segments[:, None]).astype(jnp.int32), axis=1)
    position = jnp.arange(segments.shape[0], dtype=jnp.int32) - earlier
    half = segments.shape[0] // 2
    position = jnp.where(first == 0, position, jnp.concatenate([position[half:], position[:half]]))
    half_width = head_width // 2
    frequency = jnp.exp(
        jnp.arange(half_width, dtype=jnp.float32) * (-2.0 * jnp.log(10000.0) / head_width)
    )
    angles = position.astype(jnp.float32)[:, None] * frequency[None, :]
    angles = jnp.concatenate([angles] * 4, axis=1)
    return (jnp.cos(angles), jnp.sin(angles))


def nt_dot(left, right):
    return lax.dot_general(
        left, right, (((1,), (1,)), ((), ())), preferred_element_type=jnp.float32
    )


def plain_dot(left, right):
    return jnp.dot(left, right, preferred_element_type=jnp.float32)


def key_span(block):
    return max(0, block - 2), block + 1


def pair_mask(seg_column, seg_row, first, last, block, size):
    shape = ((last - first) * size, size)
    keys = lax.broadcasted_iota(jnp.int32, shape, 0) + first * size
    rows = lax.broadcasted_iota(jnp.int32, shape, 1) + block * size
    same = seg_column[first * size : last * size, :] == seg_row[:, block * size : (block + 1) * size]
    return same & (keys <= rows)


def both_sides(values, low):
    zero = jnp.zeros_like(values)
    left_first, right_second = jnp.where(low, values, zero), jnp.where(low, zero, values)
    return (
        (left_first, pltpu.roll(left_first, HEAD_DIM, 1)),
        (pltpu.roll(right_second, HEAD_DIM, 1), right_second),
    )


def attend_body(
    at_ref,
    qkv_ref,
    cos_ref,
    sin_ref,
    seg_column_ref,
    seg_row_ref,
    out_ref,
    query_ref,
    side_ref,
    key_ref,
    value_ref,
    log_ref,
    value_turned,
):
    bf16, f32 = jnp.bfloat16, jnp.float32
    seq_len, wide = out_ref.shape
    size, twice = seq_len // 4, 2 * HEAD_DIM
    half = HEAD_DIM // 2
    pairs = wide // twice
    scale = HEAD_DIM ** (-0.5)
    at = at_ref[0]
    lane = lax.broadcasted_iota(jnp.int32, (1, twice), 1)
    low, front = lane < HEAD_DIM, lane % HEAD_DIM < half

    def place(block):
        return pl.ds(pl.multiple_of((block + 2 * at) % 4 * size, size), size)

    def turned(values, rows):
        back = pltpu.roll(values, twice - half, 1)
        ahead = pltpu.roll(values, half, 1)
        return values * cos_ref[rows, :] + jnp.where(front, -back, ahead) * sin_ref[rows, :]

    for block in range(4):
        rows, natural = place(block), slice(block * size, (block + 1) * size)
        keys = turned(qkv_ref[rows, wide : wide + twice], rows).astype(bf16)
        values = qkv_ref[rows, wide + twice : wide + 2 * twice].astype(bf16)
        key_ref[natural, :] = keys
        value_ref[natural, :] = values
        for group, sides in enumerate(both_sides(keys.astype(f32), low)):
            for side in range(2):
                side_ref[group, side, natural, :] = sides[side].astype(bf16)
        value_turned[:, natural] = values.astype(f32).T.astype(bf16)

    def pair_step(pair, carry):
        lanes = pl.ds(pl.multiple_of(pair * twice, twice), twice)
        group = pair // (pairs // 2)
        for block in range(4):
            first, last = key_span(block)
            span = slice(first * size, last * size)
            rows = place(block)
            queries = turned(qkv_ref[rows, lanes], rows).astype(bf16)
            query_ref[rows, lanes] = queries
            mask = pair_mask(seg_column_ref, seg_row_ref, first, last, block, size)
            soft = []
            for side in range(2):
                scores = nt_dot(side_ref[group, side, span, :], queries) * scale
                scores = jnp.where(mask, scores, -1e30)
                top = jnp.max(scores, axis=0, keepdims=True)
                powers = jnp.exp(scores - top)
                total = jnp.sum(powers, axis=0, keepdims=True)
                log_ref[pair, side : side + 1, block * size : (block + 1) * size] = top + jnp.log(total)
                soft.append((powers * (1.0 / total)).astype(bf16))
            weights = value_turned[pl.ds(pl.multiple_of(group * HEAD_DIM, HEAD_DIM), HEAD_DIM), span]
            result = plain_dot(weights, jnp.concatenate(soft, axis=1))
            result = jnp.concatenate([result[:, :size], result[:, size:]], axis=0)
            out_ref[rows, lanes] = result.T.astype(bf16)
        return carry

    lax.fori_loop(0, pairs, pair_step, 0)


def attend_back_body(
    at_ref,
    grad_ref,
    query_ref,
    side_ref,
    key_ref,
    value_ref,
    log_ref,
    cos_ref,
    sin_ref,
    cos_turned_ref,
    sin_turned_ref,
    seg_column_ref,
    seg_row_ref,
    out_ref,
    value_side,
    key_turned,
    key_total,
    value_total,
):
    bf16, f32 = jnp.bfloat16, jnp.float32
    seq_len, wide = query_ref.shape
    size, twice = seq_len // 4, 2 * HEAD_DIM
    half = HEAD_DIM // 2
    pairs = wide // twice
    scale = HEAD_DIM ** (-0.5)
    at = at_ref[0]
    lane = lax.broadcasted_iota(jnp.int32, (1, twice), 1)
    low, front = lane < HEAD_DIM, lane % HEAD_DIM < half

    def place(block):
        return pl.ds(pl.multiple_of((block + 2 * at) % 4 * size, size), size)

    for block in range(4):
        natural = slice(block * size, (block + 1) * size)
        for group, sides in enumerate(both_sides(value_ref[natural, :].astype(f32), low)):
            for side in range(2):
                value_side[group, side, natural, :] = sides[side].astype(bf16)
        key_turned[:, natural] = key_ref[natural, :].astype(f32).T.astype(bf16)
    key_total[...] = jnp.zeros_like(key_total)
    value_total[...] = jnp.zeros_like(value_total)

    def split(values):
        zero = jnp.zeros_like(values)
        return jnp.concatenate([jnp.where(low, values, zero), jnp.where(low, zero, values)], axis=0)

    def pair_step(pair, carry):
        lanes = pl.ds(pl.multiple_of(pair * twice, twice), twice)
        group = pair // (pairs // 2)
        for block in range(4):
            first, last = key_span(block)
            span = slice(first * size, last * size)
            rows = place(block)
            queries, grads = query_ref[rows, lanes], grad_ref[rows, lanes]
            mask = pair_mask(seg_column_ref, seg_row_ref, first, last, block, size)
            soft, slopes = [], []
            for side in range(2):
                scores = nt_dot(side_ref[group, side, span, :], queries) * scale
                logs = log_ref[pair, side : side + 1, block * size : (block + 1) * size]
                weights = jnp.exp(jnp.where(mask, scores, -1e30) - logs)
                grad_soft = nt_dot(value_side[group, side, span, :], grads)
                delta = jnp.sum(weights * grad_soft, axis=0, keepdims=True)
                slopes.append((weights * (grad_soft - delta)).astype(bf16))
                soft.append(weights.astype(bf16))
            slopes, soft = jnp.concatenate(slopes, axis=1), jnp.concatenate(soft, axis=1)
            key_total[group, span, :] += plain_dot(slopes, split(queries))
            value_total[group, span, :] += plain_dot(soft, split(grads))
            keys = key_turned[pl.ds(pl.multiple_of(group * HEAD_DIM, HEAD_DIM), HEAD_DIM), span]
            result = plain_dot(keys, slopes) * scale
            cosine, sine = cos_turned_ref[:, rows], sin_turned_ref[:, rows]
            parts = []
            for side in range(2):
                own = result[:, side * size : (side + 1) * size]
                turn = own * sine
                own = own * cosine
                parts += [own[:half] + turn[half:], own[half:] - turn[:half]]
            out_ref[rows, lanes] = jnp.concatenate(parts, axis=0).T.astype(bf16)
        return carry

    lax.fori_loop(0, pairs, pair_step, 0)

    for block in range(4):
        rows, natural = place(block), slice(block * size, (block + 1) * size)
        folded = []
        for total in (key_total, value_total):
            groups = [total[group, natural, :] for group in range(2)]
            groups = [part + pltpu.roll(part, HEAD_DIM, 1) for part in groups]
            folded.append(jnp.where(low, groups[0], groups[1]))
        keys = folded[0] * scale
        turn = keys * sin_ref[rows, :]
        back, ahead = pltpu.roll(turn, twice - half, 1), pltpu.roll(turn, half, 1)
        keys = keys * cos_ref[rows, :] + jnp.where(front, back, -ahead)
        out_ref[rows, wide : wide + twice] = keys.astype(bf16)
        out_ref[rows, wide + twice : wide + 2 * twice] = folded[1].astype(bf16)


def whole_specs(count):
    return [pl.BlockSpec(memory_space=pltpu.SMEM)] + [pl.BlockSpec(memory_space=pltpu.VMEM)] * count


def attend(tensor_at, qkv, cosine, sine, segments, heads_wide):
    seq_len, bf16, f32 = qkv.shape[0], jnp.bfloat16, jnp.float32
    twice = 2 * HEAD_DIM
    shapes = (
        ((seq_len, heads_wide), bf16),
        ((seq_len, heads_wide), bf16),
        ((2, 2, seq_len, twice), bf16),
        ((seq_len, twice), bf16),
        ((seq_len, twice), bf16),
        ((heads_wide // twice, 2, seq_len), f32),
    )
    work = heads_wide * seq_len * seq_len
    return pl.pallas_call(
        attend_body,
        in_specs=whole_specs(5),
        out_specs=[pl.BlockSpec(memory_space=pltpu.VMEM)] * len(shapes),
        out_shape=[jax.ShapeDtypeStruct(shape, kind) for shape, kind in shapes],
        scratch_shapes=[pltpu.VMEM((twice, seq_len), bf16)],
        cost_estimate=pl.CostEstimate(
            flops=4 * work, transcendentals=work // HEAD_DIM, bytes_accessed=8 * qkv.size
        ),
    )(tensor_at[None], qkv, cosine, sine, segments[:, None], segments[None, :])


def attend_back(tensor_at, grad_cat, saved, cosine, sine, segments):
    queries, sides, keys, values, logs = saved
    (seq_len, heads_wide), bf16, f32 = queries.shape, jnp.bfloat16, jnp.float32
    twice = 2 * HEAD_DIM
    work = heads_wide * seq_len * seq_len
    return pl.pallas_call(
        attend_back_body,
        in_specs=whole_specs(12),
        out_specs=pl.BlockSpec(memory_space=pltpu.VMEM),
        out_shape=jax.ShapeDtypeStruct((seq_len, heads_wide + 2 * twice), bf16),
        scratch_shapes=[
            pltpu.VMEM((2, 2, seq_len, twice), bf16),
            pltpu.VMEM((twice, seq_len), bf16),
            pltpu.VMEM((2, seq_len, twice), f32),
            pltpu.VMEM((2, seq_len, twice), f32),
        ],
        cost_estimate=pl.CostEstimate(
            flops=10 * work, transcendentals=work // HEAD_DIM, bytes_accessed=8 * queries.size
        ),
    )(
        tensor_at[None],
        grad_cat,
        queries,
        sides,
        keys,
        values,
        logs,
        cosine,
        sine,
        cosine[:, :HEAD_DIM].T,
        sine[:, :HEAD_DIM].T,
        segments[:, None],
        segments[None, :],
    )


def cost_of(flops, *arrays):
    moved = sum(array.size * jnp.dtype(array.dtype).itemsize for array in arrays)
    return pl.CostEstimate(flops=flops, transcendentals=0, bytes_accessed=moved)


def tile_of(columns, most=256):
    return next(size for size in range(most, 0, -128) if columns % size == 0)


def by_rows(rows, step, chunk=256):
    chunk = min(chunk, rows)

    def one(at, carry):
        step(pl.ds(pl.multiple_of(at * chunk, chunk), chunk))
        return carry

    lax.fori_loop(0, rows // chunk, one, 0)


def times(left, right, first, columns, kind):
    rows, depth = left.shape
    tile = tile_of(columns)
    shape = jax.ShapeDtypeStruct((rows, columns), kind)

    def body(left_ref, right_ref, out_ref):
        def step(at):
            out_ref[at, :] = plain_dot(left_ref[at, :], right_ref[...]).astype(out_ref.dtype)

        by_rows(rows, step)

    return pl.pallas_call(
        body,
        grid=(columns // tile,),
        in_specs=[
            pl.BlockSpec((rows, depth), lambda j: (0, 0)),
            pl.BlockSpec((depth, tile), lambda j: (0, j + first // tile)),
        ],
        out_specs=pl.BlockSpec((rows, tile), lambda j: (0, j)),
        out_shape=shape,
        cost_estimate=cost_of(2 * rows * depth * columns, left, shape),
    )(left, right)


def times_turned(left, at, right, first, kind):
    stack = left if left.ndim == 3 else left[None]
    parts, rows, depth = stack.shape
    rows //= 2
    count, wide = right.shape
    tile = tile_of(count, 512)

    def body(left_ref, right_ref, out_ref):
        def step(rows_at):
            total = 0.0
            for part in range(parts):
                begin = first + part * depth
                total += nt_dot(left_ref[part, rows_at, :], right_ref[:, begin : begin + depth])
            out_ref[rows_at, :] = total.astype(out_ref.dtype)

        by_rows(rows, step)

    shape = jax.ShapeDtypeStruct((rows, count), kind)
    return pl.pallas_call(
        body,
        grid=(count // tile,),
        in_specs=[
            pl.BlockSpec((parts, rows, depth), lambda j: (0, at, 0)),
            pl.BlockSpec((tile, wide), lambda j: (j, 0)),
        ],
        out_specs=pl.BlockSpec((rows, tile), lambda j: (0, j)),
        out_shape=shape,
        cost_estimate=cost_of(2 * rows * depth * parts * count, right, shape),
    )(stack, right)


def turned_times(left, half, right, received=None):
    stack = right if right.ndim == 3 else right[None]
    parts, tokens, columns = stack.shape
    count = left.shape[1] // 2
    tile = tile_of(columns, max(512, columns // 2))
    tiles = columns // tile

    def body(half_ref, left_ref, right_ref, *rest):
        *received_ref, out_ref, turned = rest

        @pl.when(pl.program_id(0) == 0)
        def _():
            def turn(at, carry):
                columns_at = pl.ds(pl.multiple_of(at * 128, 128), 128)
                turned[columns_at, :] = left_ref[:, columns_at].astype(jnp.float32).T.astype(jnp.bfloat16)
                return carry

            lax.fori_loop(0, count // 128, turn, 0)

        def step(at):
            total = plain_dot(turned[at, :], right_ref[0])
            if received_ref:
                total += received_ref[0][at, :].astype(jnp.float32)
            out_ref[at, :] = total.astype(jnp.bfloat16)

        by_rows(count, step)

    block = pl.BlockSpec((count, tile), lambda j, half_ref: (0, j))
    shape = jax.ShapeDtypeStruct((count, parts * columns), jnp.bfloat16)
    more = [] if received is None else [received]
    return pl.pallas_call(
        body,
        grid_spec=pltpu.PrefetchScalarGridSpec(
            num_scalar_prefetch=1,
            grid=(parts * tiles,),
            in_specs=[
                pl.BlockSpec((tokens, count), lambda j, half_ref: (0, half_ref[0])),
                pl.BlockSpec((1, tokens, tile), lambda j, half_ref: (j // tiles, 0, j % tiles)),
            ]
            + [block] * len(more),
            out_specs=block,
            scratch_shapes=[pltpu.VMEM((count, tokens), jnp.bfloat16)],
        ),
        out_shape=shape,
        cost_estimate=cost_of(2 * tokens * count * parts * columns, stack, shape, *more),
    )(half[None], left, stack, *more)


def feed_forward(hidden, gate_up_all):
    rows, depth = hidden.shape
    wide = gate_up_all.shape[1] // 2
    tile = tile_of(wide)

    def body(hidden_ref, gate_ref, up_ref, gate_out, up_out, active_out):
        def step(at):
            gate_part = plain_dot(hidden_ref[at, :], gate_ref[...])
            upward = plain_dot(hidden_ref[at, :], up_ref[...])
            gate_out[at, :] = gate_part
            up_out[at, :] = upward
            active_out[at, :] = (gate_part * jax.nn.sigmoid(gate_part) * upward).astype(jnp.bfloat16)

        by_rows(rows, step)

    block = pl.BlockSpec((rows, tile), lambda j: (0, j))
    kinds = (jnp.float32, jnp.float32, jnp.bfloat16)
    shapes = [jax.ShapeDtypeStruct((rows, wide), kind) for kind in kinds]
    return pl.pallas_call(
        body,
        grid=(wide // tile,),
        in_specs=[
            pl.BlockSpec((rows, depth), lambda j: (0, 0)),
            pl.BlockSpec((depth, tile), lambda j: (0, j)),
            pl.BlockSpec((depth, tile), lambda j: (0, j + wide // tile)),
        ],
        out_specs=[block] * 3,
        out_shape=shapes,
        cost_estimate=cost_of(4 * rows * depth * wide, gate_up_all, *shapes),
    )(hidden, gate_up_all, gate_up_all)


def feed_forward_back(cot, down_all, gate_part, upward):
    rows, depth = cot.shape
    wide = down_all.shape[1]
    tile = tile_of(wide, wide // 2)

    def body(cot_ref, down_ref, gate_ref, up_ref, out_ref):
        def step(at):
            grad_act = plain_dot(cot_ref[at, :], down_ref[...])
            gate = gate_ref[at, :]
            sigmoid_gate = jax.nn.sigmoid(gate)
            slope = sigmoid_gate * (1.0 + gate * (1.0 - sigmoid_gate))
            out_ref[0, at, :] = (grad_act * up_ref[at, :] * slope).astype(jnp.bfloat16)
            out_ref[1, at, :] = (grad_act * (gate * sigmoid_gate)).astype(jnp.bfloat16)

        by_rows(rows, step)

    block = pl.BlockSpec((rows, tile), lambda j: (0, j))
    shape = jax.ShapeDtypeStruct((2, rows, wide), jnp.bfloat16)
    return pl.pallas_call(
        body,
        grid=(wide // tile,),
        in_specs=[
            pl.BlockSpec((rows, depth), lambda j: (0, 0)),
            pl.BlockSpec((depth, tile), lambda j: (0, j)),
            block,
            block,
        ],
        out_specs=pl.BlockSpec((2, rows, tile), lambda j: (0, 0, j)),
        out_shape=shape,
        cost_estimate=cost_of(2 * rows * depth * wide, down_all, gate_part, upward, shape),
    )(cot, down_all, gate_part, upward)


def adam_step(parameter, gradient, first_moment, second_moment):
    new_first = beta_one * first_moment + (1.0 - beta_one) * gradient
    new_second = beta_two * second_moment + (1.0 - beta_two) * gradient * gradient
    corrected_first = new_first / (1.0 - beta_one**step_count)
    corrected_second = new_second / (1.0 - beta_two**step_count)
    new_parameter = parameter - lr_rate * (
        corrected_first / (jnp.sqrt(corrected_second) + adam_eps) + decay_rate * parameter
    )
    return (new_parameter, new_first, new_second)


def pack(*weights):
    rows = weights[0].shape[0]
    wide = sum(weight.size // rows for weight in weights)

    def body(*refs):
        *weight_refs, out_ref = refs
        begin = 0
        for ref in weight_refs:
            for part in range(ref.shape[1]) if len(ref.shape) == 3 else (None,):
                values = ref[...] if part is None else ref[:, part, :]
                out_ref[:, begin : begin + ref.shape[-1]] = values.astype(jnp.bfloat16)
                begin += ref.shape[-1]

    shape = jax.ShapeDtypeStruct((rows, wide), jnp.bfloat16)
    return pl.pallas_call(
        body,
        in_specs=[pl.BlockSpec(memory_space=pltpu.VMEM)] * len(weights),
        out_specs=pl.BlockSpec(memory_space=pltpu.VMEM),
        out_shape=shape,
        cost_estimate=cost_of(shape.size, shape, *weights),
    )(*weights)


def adam_update(gradient, parameters, firsts, seconds, chunk):
    rows = gradient.shape[0]
    chunk = min(rows, chunk)
    count = len(parameters)

    def body(gradient_ref, *refs):
        old, new = refs[: 3 * count], refs[3 * count :]
        begin = 0
        for at in range(count):
            shape = old[3 * at].shape
            middle = range(shape[1]) if len(shape) == 3 else (None,)
            for part in middle:
                wide = shape[-1]
                where = (slice(None), slice(None)) if part is None else (slice(None), part, slice(None))
                grads = gradient_ref[:, begin : begin + wide].astype(jnp.float32)
                begin += wide
                results = adam_step(
                    old[3 * at][where], grads, old[3 * at + 1][where], old[3 * at + 2][where]
                )
                new[4 * at][where] = grads
                for index, result in enumerate(results):
                    new[4 * at + 1 + index][where] = result

    def spec(array):
        return pl.BlockSpec(
            (chunk,) + array.shape[1:], lambda i, zeros=(0,) * (array.ndim - 1): (i,) + zeros
        )

    inputs = [array for group in zip(parameters, firsts, seconds) for array in group]
    outputs = [array for array in parameters for _ in range(4)]
    results = pl.pallas_call(
        body,
        grid=(rows // chunk,),
        in_specs=[spec(gradient)] + [spec(array) for array in inputs],
        out_specs=[spec(array) for array in outputs],
        out_shape=[jax.ShapeDtypeStruct(array.shape, jnp.float32) for array in outputs],
        cost_estimate=cost_of(20 * gradient.size, *inputs, *outputs),
    )(gradient, *inputs)
    return [results[4 * at : 4 * at + 4] for at in range(count)]


def make_shards(dp_size):
    order = ring_order(dp_size)
    inverse_order = [order.index(i) for i in range(dp_size)]
    chips = dp_size // 2
    rings = [order[:chips], order[chips:]]

    def gather(values):
        return lax.all_gather(values, "dp", axis=0, tiled=True, axis_index_groups=[order])

    def scatter(values):
        return lax.psum_scatter(
            values, "dp", scatter_dimension=0, tiled=True, axis_index_groups=rings
        )

    def swap_core(values):
        return lax.ppermute(values, "dp", [(i, i ^ 1) for i in range(dp_size)])

    def halve_scatter(values):
        place = jnp.asarray(inverse_order, jnp.int32)[lax.axis_index("dp")] % chips
        rest = values.reshape(2, chips // 2, -1, values.shape[1]).astype(jnp.float32)

        def halved(first, second, upper, mask):
            keep, send = jnp.where(upper, second, first), jnp.where(upper, first, second)
            pairs = [(ring[i], ring[i ^ mask]) for ring in rings for i in range(chips)]
            received = lax.ppermute(send.astype(jnp.bfloat16), "dp", pairs)
            return keep + received.astype(jnp.float32)

        rest = halved(rest[0], rest[1], place >= chips // 2, chips - 1)
        bit = 1
        while bit < chips // 2:
            rest = rest.reshape(rest.shape[0] // 2, 2, *rest.shape[1:])
            rest = halved(rest[:, 0], rest[:, 1], place // bit % 2 == 1, bit)
            bit *= 2
        return rest[0].astype(jnp.bfloat16)

    def pair_grad(left, right):
        core = lax.axis_index("dp") % 2
        other = turned_times(left, 1 - core, right)
        received = swap_core(other)
        return turned_times(left, core, right, received)

    def swap(values):
        return lax.ppermute(values, "tensor", [(0, 1), (1, 0)])

    def gather_small(values):
        at = lax.axis_index("dp")
        place = jnp.asarray(inverse_order, jnp.int32)[at]
        slots = lax.broadcasted_iota(jnp.int32, (1, dp_size, 1), 1) == place
        total = jnp.where(slots, values[:, None, :], jnp.zeros((), values.dtype))
        step = 1
        while step < dp_size:
            total = total + lax.ppermute(total, "dp", [(i, i ^ step) for i in range(dp_size)])
            step *= 2
        return total.reshape(values.shape[0], -1)

    def shards(
        block_input,
        segment_ids,
        cotangent,
        attn_gain,
        query_weight,
        key_value_weight,
        out_weight,
        feed_gain,
        gate_up_weight,
        down_weight,
        *moments,
    ):
        bf16, f32 = jnp.bfloat16, jnp.float32
        rows = attn_gain.shape[0]
        own = block_input.shape[0]
        heads_wide = query_weight.shape[1]
        keys_wide = key_value_weight.shape[2]
        tensor_at = lax.axis_index("tensor")

        qkv_wide = heads_wide + 2 * keys_wide
        gains = gather_small(jnp.stack([attn_gain, feed_gain]).astype(bf16)).astype(f32)
        attn_all = gather(pack(query_weight, key_value_weight, out_weight))
        gate_up_all = gather(gate_up_weight.astype(bf16).reshape(rows, -1))
        down_all = gather(down_weight.astype(bf16))
        gain_one, gain_two = gains[0:1], gains[1:2]

        block_rows = permute_blocks(block_input, order)
        cot_own = permute_blocks(cotangent, order)
        segments = segment_ids[0]
        cosine_table, sine_table = rotary_tables(segments, HEAD_DIM, tensor_at * own)

        def both(values):
            return jnp.concatenate([values, swap(values)], axis=0)

        def summed(left, right, first):
            partial = times_turned(left, 1, right, first, bf16)
            theirs = swap(partial)
            mine = times_turned(left, 0, right, first, f32)
            return mine + theirs.astype(f32)

        normed_one, inverse_one = norm_parts(block_rows)
        hidden_one = both((normed_one * gain_one).astype(bf16))
        cot_rows = both(cot_own.astype(bf16))

        qkv = times(hidden_one, attn_all, 0, qkv_wide, f32)
        attn_cat, *saved = attend(
            tensor_at, qkv, cosine_table, sine_table, segments, heads_wide
        )

        residual = block_rows + summed(attn_cat, attn_all, qkv_wide)
        normed_two, inverse_two = norm_parts(residual)
        hidden_two = both((normed_two * gain_two).astype(bf16))
        gate_part, upward, activated = feed_forward(hidden_two, gate_up_all)
        down_grad = pair_grad(cot_rows, activated)
        down_grad, down_all = lax.optimization_barrier((down_grad, down_all))
        down_sum = scatter(down_grad)
        grad_gate_up = feed_forward_back(cot_rows, down_all, gate_part, upward)
        grad_hidden_two = summed(grad_gate_up, gate_up_all, 0)
        gate_up_grad = pair_grad(hidden_two, grad_gate_up)
        gate_up_sum = scatter(gate_up_grad)
        feed_sum = summed(activated, down_all, 0)
        block_output = lax.optimization_barrier(residual) + feed_sum
        grad_residual = cot_own + norm_back(grad_hidden_two, gain_two, normed_two, inverse_two)
        feed_gain_part = jnp.sum(grad_hidden_two * normed_two, axis=0)
        grad_rows = both(grad_residual.astype(bf16))
        out_grad = pair_grad(grad_rows, attn_cat)
        grad_cat = times(grad_rows, attn_all, qkv_wide, heads_wide, bf16)
        grad_qkv = attend_back(
            tensor_at, grad_cat, saved, cosine_table, sine_table, segments
        )
        grad_hidden_one = summed(grad_qkv, attn_all, 0)
        qkv_grad = pair_grad(hidden_one, grad_qkv)
        input_grad = grad_residual + norm_back(grad_hidden_one, gain_one, normed_one, inverse_one)
        attn_gain_part = jnp.sum(grad_hidden_one * normed_one, axis=0)

        parts = [rows_major(qkv_grad[:, :heads_wide]), rows_major(out_grad)]
        attn_sum = rows_major(scatter(jnp.concatenate(parts, axis=1)))
        key_value_grad = qkv_grad[:, heads_wide:]
        if chips & (chips - 1):
            key_value_sum = scatter(key_value_grad)
        else:
            key_value_sum = halve_scatter(key_value_grad)

        gain_parts = jnp.stack([attn_gain_part, feed_gain_part])
        gain_parts = gain_parts + swap(gain_parts)
        step = 1
        while step < dp_size:
            pairs = [(i, i ^ step) for i in range(dp_size)]
            gain_parts = gain_parts + lax.ppermute(gain_parts, "dp", pairs)
            step *= 2
        place = jnp.asarray(inverse_order, jnp.int32)[lax.axis_index("dp")]
        gain_sums = lax.dynamic_slice(gain_parts, (0, place * rows), (2, rows))
        attn_gain_sum, feed_gain_sum = gain_sums[0], gain_sums[1]

        count = len(moments) // 2
        firsts, seconds = moments[:count], moments[count:]

        def update(gradient, parameters, places, chunk):
            results = adam_update(
                gradient,
                parameters,
                [firsts[at] for at in places],
                [seconds[at] for at in places],
                chunk,
            )
            return dict(zip(places, results))

        attn_parameters = (query_weight, out_weight)
        results = update(down_sum, (down_weight,), (6,), 32)
        results |= update(gate_up_sum, (gate_up_weight,), (5,), 16)
        results |= update(attn_sum, attn_parameters, (1, 3), 64)
        results |= update(key_value_sum, (key_value_weight,), (2,), 64)
        for at, parameter, gradient in (
            (0, attn_gain, attn_gain_sum),
            (4, feed_gain, feed_gain_sum),
        ):
            results[at] = (gradient, *adam_step(parameter, gradient, firsts[at], seconds[at]))
        return (
            permute_blocks(block_output, inverse_order),
            permute_blocks(input_grad, inverse_order),
        ) + tuple(results[at][kind] for kind in range(4) for at in range(count))

    return shards


def solution(mesh):
    tokens = P(("dp", "tensor"), None)
    gain = P("dp")
    flat = P("dp", "tensor")
    paired = P("dp", None, "tensor")
    weights = (gain, flat, paired, flat, gain, paired, flat)
    shards = make_shards(mesh.shape["dp"])

    return jax.shard_map(
        shards,
        mesh=mesh,
        in_specs=(tokens, P("dp", None), tokens) + weights * 3,
        out_specs=(tokens, tokens) + weights * 4,
        check_vma=False,
    )
```
